256 devices in a mesh: seq: 64 (over x, y, z_hi, core), tp: 4 (over z_lo).
Axes of the slice: x: 4, y: 4, z: 8 (z_hi: 2, z_lo: 4; z = z_hi * 4 + z_lo), core: 2. Of those that a mesh axis runs over, the one named last changes fastest.
Arguments:
- hidden: bfloat16 [64, 512, 2048], P('seq', 'tp'), may hold values from -6 to 6
- norm_gain: bfloat16 [2048], replicated, may hold values from 0.099609375 to 1.8984375
- qkv_weight: bfloat16 [2048, 3, 2048], P(None, None, 'tp'), may hold values from -0.0625 to 0.0625
- out_weight: bfloat16 [2048, 2048], P('tp'), may hold values from -0.25 to 0.25
- bias_table: float32 [32, 32], P(None, 'tp'), may hold values from -4 to 4
- prefix_cache: bfloat16 [512, 2, 2048], P('seq', None, 'tp'), may hold values from -64 to 64
- suffix_lengths: int32 [64], replicated, may hold values from 64 to 512, as said below
- request_of_slot: int32 [64], replicated, may hold values from 0 to 63, each once
- block_of_slot: int32 [64], replicated, may hold values from 0 to 63, each once
- bias_bucket: int32 [640], replicated, may hold values from 0 to 31
Outputs:
- attended: bfloat16 [64, 512, 2048], P('seq', 'tp')
The draws below stay inside these ranges and needn't reach their ends.
Inputs may be any that keep to these rules, and one draw needn't show every extreme that they name: `suffix_lengths`: every suffix holds 64 to 512 tokens, and some request holds exactly 512.
All inputs are finite; a program needn't handle non-finite values.
Results may differ from the reference program's by a relative error of at most 0.012.
The reference program's roundings to bfloat16 on the way count: a program that leaves them out, or rounds other values in their place, can miss the bound.
Values may be sent and summed in bfloat16 or wider, within the bound.
A program may use at most 320 MiB of HBM per device.

```python
import jax
import jax.numpy as jnp
from jax import lax

D = 2048
H = 32
DH = 64
NB = 32
LMAX = 512
PB = 8
R = 64
RG = 16
NBG = 16
PREFIX = 128
CACHE = 512
DIST = 640
HD = 2048
N_SEQ = 64


def draw_suffix_lengths(key, part):
    first, second = jax.random.split(jax.random.fold_in(key, 11))
    values = jax.random.randint(first, (R,), LMAX // 8, LMAX + 1)
    chosen = jax.random.randint(second, (), 0, R)
    return jnp.where(jnp.arange(R) == chosen, LMAX, values).astype(jnp.int32)


def draw_prefix_cache(key, part):
    first, second = jax.random.split(jax.random.fold_in(key, 23), 2)
    key_part = jnp.clip(0.5 * jax.random.normal(first, (CACHE, HD), jnp.float32), -3.0, 3.0)
    value_part = jnp.clip(jax.random.normal(second, (CACHE, HD), jnp.float32), -6.0, 6.0)
    return jnp.stack([key_part, value_part], 1).astype(jnp.bfloat16)


def touch_ends(drawn, stream_key, least, top_value):
    index_at = [jax.random.randint(jax.random.fold_in(stream_key, axis), (), 0, length) for axis, length in enumerate(drawn.shape)]
    main_axis = drawn.shape.index(max(drawn.shape))
    next_to = index_at[:main_axis] + [(index_at[main_axis] + 1) % drawn.shape[main_axis]] + index_at[main_axis + 1:]
    return drawn.at[tuple(index_at)].set(least).at[tuple(next_to)].set(top_value)


def levels(key, shape, pieces, low, high):
    gain, own = 1.0, jax.random.fold_in(key, 6)
    for dim, blocks in pieces:
        steps = jnp.exp(jax.random.uniform(jax.random.fold_in(own, dim), (blocks,), jnp.float32, low / len(pieces), high / len(pieces)))
        gain = gain * jnp.repeat(steps, shape[dim] // blocks).reshape([-1 if axis == dim else 1 for axis in range(len(shape))])
    return gain


def bell_draw(rng, dims, deviation, reach, cuts=(), held_as=jnp.bfloat16):
    gain = levels(rng, dims, cuts, -0.22, 0.18) if cuts else 1.0
    drawn = jax.random.normal(rng, dims, jnp.float32) * deviation * gain
    return jnp.minimum(jnp.maximum(drawn, -reach), reach).astype(held_as)


def setup_inputs(seed: int = 0) -> dict:
    keys = jax.random.split(jax.random.key(seed), 11)
    return {
        "hidden": bell_draw(keys[0], (R, LMAX, D), 1.0, 6.0, ((0, 64), (1, 4))),
        "norm_gain": jnp.clip(1.0 + 0.18 * jax.random.normal(keys[1], (D,), jnp.float32), 0.099609375, 1.8984375).astype(jnp.bfloat16),
        "qkv_weight": bell_draw(keys[2], (D, 3, HD), (4 * D) ** -0.5, 0.0625, ((2, 4),)),
        "out_weight": bell_draw(keys[3], (HD, D), (HD // 4) ** -0.5, 0.25, ((0, 4),)),
        "bias_table": bell_draw(keys[4], (NB, H), 1.0, 4.0, ((1, 4),), jnp.float32),
        "prefix_cache": draw_prefix_cache(jax.random.fold_in(keys[10], 71), 0),
        "suffix_lengths": draw_suffix_lengths(jax.random.fold_in(keys[10], 71), 0),
        "request_of_slot": jax.random.permutation(keys[7], R).astype(jnp.int32),
        "block_of_slot": jax.random.permutation(keys[8], N_SEQ).astype(jnp.int32),
        "bias_bucket": touch_ends(jax.random.randint(keys[9], (DIST,), 0, NB), jax.random.fold_in(keys[9], 1), 0, NB - 1).astype(jnp.int32),
    }


def reference(hidden, norm_gain, qkv_weight, out_weight, bias_table, prefix_cache, suffix_lengths, request_of_slot, block_of_slot, bias_bucket):
    bias_dist = jnp.take(bias_table, bias_bucket, axis=0)
    cache_rows = jnp.arange(CACHE, dtype=jnp.int32)
    cache_block = jnp.take(block_of_slot, cache_rows // PB)
    cache_group = cache_block // NBG
    cache_pos = cache_block % NBG * PB + cache_rows % PB
    cache_keys = prefix_cache[:, 0, :]
    cache_values = prefix_cache[:, 1, :]
    weights = qkv_weight.reshape(D, 3 * HD)
    positions = jnp.arange(LMAX, dtype=jnp.int32)

    def one_slot(slot):
        request = jnp.take(request_of_slot, slot)
        group = request // RG
        length = jnp.take(suffix_lengths, request)
        states = lax.dynamic_index_in_dim(hidden, slot, 0, keepdims=False).astype(jnp.float32)
        normed = (states * lax.rsqrt(lax.optimization_barrier(jnp.mean(states * states, -1, keepdims=True)) + 1e-06) * norm_gain.astype(jnp.float32)).astype(jnp.bfloat16)
        qkv = jnp.dot(normed, weights, preferred_element_type=jnp.float32).astype(jnp.bfloat16)
        query = qkv[:, :HD]
        key_rows = jnp.concatenate([cache_keys, qkv[:, HD:2 * HD]], 0)
        value_rows = jnp.concatenate([cache_values, qkv[:, 2 * HD:]], 0)
        key_pos = jnp.concatenate([cache_pos, PREFIX + positions])
        key_ok = jnp.concatenate([cache_group == group, jnp.ones((LMAX,), bool)])
        distance = (PREFIX + positions)[:, None] - key_pos[None, :]
        allowed = key_ok[None, :] & (distance >= 0)
        distance = jnp.clip(distance, 0, DIST - 1)
        query_heads = query.reshape(LMAX, H, DH).transpose(1, 0, 2)
        key_heads = key_rows.reshape(-1, H, DH).transpose(1, 0, 2)
        value_heads = value_rows.reshape(-1, H, DH).transpose(1, 0, 2)

        def one_head(items):
            query_one, key_one, value_one, bias_row = items
            scores = jnp.dot(query_one, key_one.T, preferred_element_type=jnp.float32) + jnp.take(bias_row, distance)
            scores = jnp.where(allowed, scores, -jnp.inf)
            highest = lax.optimization_barrier(jnp.max(scores, -1, keepdims=True))
            probs = jnp.exp(scores - highest)
            denom = lax.optimization_barrier(jnp.sum(probs, -1, keepdims=True))
            return jnp.dot(probs.astype(jnp.bfloat16), value_one, preferred_element_type=jnp.float32) / denom
        head_out = lax.map(one_head, (query_heads, key_heads, value_heads, bias_dist.T))
        attn = head_out.transpose(1, 0, 2).reshape(LMAX, HD).astype(jnp.bfloat16)
        projected = jnp.dot(attn, out_weight, preferred_element_type=jnp.float32)
        return jnp.where((positions < length)[:, None], projected, 0.0).astype(jnp.bfloat16)
    return lax.map(one_slot, jnp.arange(R, dtype=jnp.int32))
```

```python
import functools

import jax
import jax.numpy as jnp
from jax import lax
from jax.experimental import pallas as pl
from jax.experimental.pallas import tpu as pltpu
from jax.sharding import PartitionSpec as P

MESH = pl.DeviceIdType.MESH
TP = 4
ROWS = 128
SLOT = ROWS * TP
D = 2048
COLS = 512
HEADS = 8
PB = 8
PREFIX = 128
DIST = 640
BUCKETS = 32
GROUPS = 4
GROUP_BLOCKS = 16
NEG = -1e30
CH = 4
CROWS = ROWS // CH


def position():
    s = lax.axis_index("seq")
    t = lax.axis_index("tp")
    return s // 16, lax.rem(s // 4, 4), lax.rem(s // 2, 2), lax.rem(s, 2), t


def place(x, y, zh, c, t):
    return (((x * 4 + y) * 2 + zh) * 2 + c, t)


def gather_kernel(hid, gain_ref, w_hbm, pref_ref, qkv_ref, pbuf, wv, hbuf, kvown, own_sem, w_sem, ss, rs, pss, prs):
    x, y, zh, c, t = position()
    zz = zh * 4 + t

    def along_z(step):
        other = lax.rem(zz + step + 8, 8)
        return place(x, y, other // 4, c, lax.rem(other, 4))

    right, left = along_z(1), along_z(-1)
    half = place(x, y, 1 - zh, c, t)
    xs = (place(lax.rem(x + 1, 4), y, zh, c, t), place(lax.rem(x + 3, 4), y, zh, c, t))
    ys = (place(x, lax.rem(y + 1, 4), zh, c, t), place(x, lax.rem(y + 3, 4), zh, c, t))
    core = place(x, y, zh, 1 - c, t)
    partners = (right, left, half, *xs, *ys, core)
    barrier = pltpu.get_barrier_semaphore()
    for partner in partners:
        pl.semaphore_signal(barrier, inc=1, device_id=partner, device_id_type=MESH)
    load_own = pltpu.make_async_copy(hid, hbuf.at[pl.ds(pl.multiple_of(t * ROWS, ROWS), ROWS)], own_sem.at[0])
    load_own.start()
    load_w = [pltpu.make_async_copy(w_hbm.at[i], wv.at[i], w_sem.at[i]) for i in range(3)]
    for copy in load_w:
        copy.start()
    both = pref_ref[...].astype(jnp.float32)
    kvown[0] = both[:, 0, :].astype(jnp.bfloat16)
    kvown[1] = both[:, 1, :].astype(jnp.bfloat16)
    pl.semaphore_wait(barrier, len(partners))

    def piece(shard, j):
        return pl.ds(pl.multiple_of(shard * ROWS + j * CROWS, CROWS), CROWS)

    def hop(way, k, j):
        shard = t - k if way == 0 else t + k
        source = hid.at[pl.ds(j * CROWS, CROWS)] if k == 0 else hbuf.at[piece(shard, j)]
        return pltpu.make_async_remote_copy(
            src_ref=source,
            dst_ref=hbuf.at[piece(shard, j)],
            send_sem=ss.at[way, k, j],
            recv_sem=rs.at[way, k, j],
            device_id=right if way == 0 else left,
            device_id_type=MESH,
        )

    def sends(way, k):
        return (t < TP - 1) & (t - k >= 0) if way == 0 else (t > 0) & (t + k < TP)

    def gets(way, k):
        return t - k >= 0 if way == 0 else t + k < TP

    for j in range(CH):
        for way in range(2):
            @pl.when(sends(way, 0))
            def _():
                hop(way, 0, j).start()

    def remote(index, src, dst, to):
        return pltpu.make_async_remote_copy(
            src_ref=src, dst_ref=dst, send_sem=pss.at[index], recv_sem=prs.at[index], device_id=to, device_id_type=MESH
        )

    mine = pbuf.at[c, y, x, zh]
    local = pltpu.make_async_copy(kvown, mine, own_sem.at[1])
    local.start()
    swap = remote(0, kvown, mine, half)
    swap.start()

    def ring(base, view, part, me, peers):
        ahead, behind = lax.rem(me + 1, 4), lax.rem(me + 3, 4)

        def first():
            for k in range(2):
                remote(base + k, view(me), view(me), peers[k]).start()

        def arrived():
            remote(base, view(behind), view(behind), peers[0]).wait_recv()
            remote(base + 1, view(ahead), view(ahead), peers[1]).wait_recv()

        def second():
            remote(base + 2, part(behind, 0), part(behind, 0), peers[0]).start()
            remote(base + 3, part(ahead, 1), part(ahead, 1), peers[1]).start()

        def complete():
            far = lax.rem(me + 2, 4)
            remote(base + 2, part(far, 0), part(far, 0), peers[0]).wait_recv()
            remote(base + 3, part(far, 1), part(far, 1), peers[1]).wait_recv()

        def drain():
            for k in range(2):
                remote(base + k, view(me), view(me), peers[k]).wait_send()
            remote(base + 2, part(behind, 0), part(behind, 0), peers[0]).wait_send()
            remote(base + 3, part(ahead, 1), part(ahead, 1), peers[1]).wait_send()

        return first, arrived, second, complete, drain

    ring_x = ring(1, lambda i: pbuf.at[c, y, i], lambda i, h: pbuf.at[c, y, i, h], x, xs)
    ring_y = ring(5, lambda i: pbuf.at[c, i], lambda i, h: pbuf.at[c, i, pl.ds(2 * h, 2)], y, ys)
    swap_core = remote(9, pbuf.at[c], pbuf.at[c], core)

    def project(shard):
        rows = pl.ds(pl.multiple_of(shard * ROWS, ROWS), ROWS)
        states = hbuf[rows, :].astype(jnp.float32)
        scale = lax.rsqrt(jnp.mean(states * states, -1, keepdims=True) + 1e-06)
        normed = (states * scale * gain_ref[...].astype(jnp.float32)).astype(jnp.bfloat16)
        for i in range(3):
            qkv_ref[rows, i * COLS : (i + 1) * COLS] = jnp.dot(
                normed, wv[i], preferred_element_type=jnp.float32
            ).astype(jnp.bfloat16)

    def pass_on(k, j):
        for way in range(2):
            @pl.when(gets(way, k))
            def _():
                shard = t - k if way == 0 else t + k
                pltpu.make_async_remote_copy(
                    src_ref=hbuf.at[piece(shard, j)],
                    dst_ref=hbuf.at[piece(shard, j)],
                    send_sem=ss.at[way, k - 1, j],
                    recv_sem=rs.at[way, k - 1, j],
                    device_id=right if way == 0 else left,
                    device_id_type=MESH,
                ).wait_recv()

            @pl.when(sends(way, k))
            def _():
                hop(way, k, j).start()

    def order(i):
        ends = jnp.where(t == 0, i, TP - 1 - i)
        inner = jnp.where(t == 1, (0, 2, 3)[i - 1], (3, 1, 0)[i - 1])
        return jnp.where((t == 0) | (t == TP - 1), ends, inner)

    load_own.wait()
    for copy in load_w:
        copy.wait()
    project(t)
    swap.wait_recv()
    local.wait()
    ring_x[0]()
    pass_on(1, 0)
    ring_x[1]()
    ring_x[2]()
    pass_on(1, 1)
    ring_x[3]()
    ring_y[0]()
    pass_on(1, 2)
    pass_on(1, 3)
    ring_y[1]()
    ring_y[2]()
    project(order(1))
    pass_on(2, 0)
    ring_y[3]()
    swap_core.start()
    pass_on(2, 1)
    pass_on(2, 2)
    pass_on(2, 3)
    project(order(2))
    for j in range(CH):
        pass_on(3, j)
    project(order(3))
    remote(9, pbuf.at[1 - c], pbuf.at[1 - c], core).wait_recv()
    swap.wait_send()
    ring_x[4]()
    ring_y[4]()
    swap_core.wait_send()
    for k in range(TP):
        for j in range(CH):
            for way in range(2):
                if k == TP - 1:
                    continue

                @pl.when(sends(way, k))
                def _():
                    hop(way, k, j).wait_send()


def gather(hidden, gain, weights, prefix):
    vmem, hbm = pl.BlockSpec(memory_space=pltpu.VMEM), pl.BlockSpec(memory_space=pl.ANY)
    return pl.pallas_call(
        gather_kernel,
        name="gather",
        out_shape=(
            jax.ShapeDtypeStruct((SLOT, 3 * COLS), jnp.bfloat16),
            jax.ShapeDtypeStruct((2, 4, 4, 2, 2, PB, COLS), jnp.bfloat16),
        ),
        in_specs=[hbm, vmem, hbm, vmem],
        out_specs=(vmem, hbm),
        scratch_shapes=[
            pltpu.VMEM((3, D, COLS), jnp.bfloat16),
            pltpu.VMEM((SLOT, D), jnp.bfloat16),
            pltpu.VMEM((2, PB, COLS), jnp.bfloat16),
            pltpu.SemaphoreType.DMA((2,)),
            pltpu.SemaphoreType.DMA((3,)),
            pltpu.SemaphoreType.DMA((2, TP, CH)),
            pltpu.SemaphoreType.DMA((2, TP, CH)),
            pltpu.SemaphoreType.DMA((10,)),
            pltpu.SemaphoreType.DMA((10,)),
        ],
        compiler_params=pltpu.CompilerParams(collective_id=0, has_side_effects=True, vmem_limit_bytes=48 << 20),
    )(hidden, gain, weights, prefix)


def attention_kernel(request_ref, block_ref, qkv_ref, pbuf, bucket_ref, table_ref, attn_ref, inverse, pre, bias, tiles, sem):
    s = lax.axis_index("seq")
    group = request_ref[s] // GROUP_BLOCKS

    def note(i, carry):
        inverse[block_ref[i]] = i
        return carry

    lax.fori_loop(0, GROUPS * GROUP_BLOCKS, note, 0)
    copies = []
    for j in range(GROUP_BLOCKS):
        owner = inverse[group * GROUP_BLOCKS + j]
        c, zh, y, x = lax.rem(owner, 2), lax.rem(owner // 2, 2), lax.rem(owner // 4, 4), owner // 16
        copy = pltpu.make_async_copy(pbuf.at[((c * 4 + y) * 4 + x) * 2 + zh], pre.at[j], sem.at[j])
        copy.start()
        copies.append(copy)

    bucket = jnp.broadcast_to(bucket_ref[...], (HEADS, DIST))
    row = jnp.zeros((HEADS, DIST), jnp.float32)
    for b in range(BUCKETS):
        row = jnp.where(bucket == b, table_ref[:, b : b + 1], row)
    bias[:, :PREFIX] = jnp.full((HEADS, PREFIX), NEG, jnp.float32)
    bias[:, PREFIX:] = row
    for h in range(HEADS):
        for delta in range(5):
            window = jnp.broadcast_to(bias[h : h + 1, delta * 128 : delta * 128 + 256], (128, 256))
            rolled = pltpu.roll(window, 0, 1, stride=1, stride_axis=0)
            tiles[h // 2, delta, :, (h % 2) * 128 : (h % 2) * 128 + 128] = rolled[:, 128:]
    for copy in copies:
        copy.wait()

    low = lax.broadcasted_iota(jnp.int32, (128, 128), 1) < 64
    for p in range(HEADS // 2):
        lanes = slice(p * 128, p * 128 + 128)

        def prefix(which):
            parts = [pre[j, which, :, lanes].astype(jnp.float32) for j in range(GROUP_BLOCKS)]
            return jnp.concatenate(parts, 0).astype(jnp.bfloat16)

        keys = jnp.concatenate([prefix(0), qkv_ref[:, COLS + p * 128 : COLS + p * 128 + 128]], 0)
        values = jnp.concatenate([prefix(1), qkv_ref[:, 2 * COLS + p * 128 : 2 * COLS + p * 128 + 128]], 0)
        values_t = values.T
        for r in range(TP):
            query = qkv_ref[r * 128 : r * 128 + 128, lanes]
            zero = jnp.zeros_like(query)
            stacked = jnp.concatenate([jnp.where(low, query, zero), jnp.where(low, zero, query)], 0)
            blocks = []
            for kb in range(r + 2):
                part = lax.dot_general(
                    keys[kb * 128 : kb * 128 + 128], stacked, (((1,), (1,)), ((), ())), preferred_element_type=jnp.float32
                )
                blocks.append(part + tiles[p, r + 1 - kb])
            top = functools.reduce(jnp.maximum, [jnp.max(b, 0, keepdims=True) for b in blocks])
            probs = [jnp.exp(b - top) for b in blocks]
            denom = functools.reduce(jnp.add, [jnp.sum(b, 0, keepdims=True) for b in probs])
            probs = jnp.concatenate([b.astype(jnp.bfloat16) for b in probs], 0)
            out = jnp.dot(values_t[:, : (r + 2) * 128], probs, preferred_element_type=jnp.float32) / denom
            pair = jnp.concatenate([out[:64, :128], out[64:, 128:]], 0)
            attn_ref[r * 128 : r * 128 + 128, lanes] = pair.T.astype(jnp.bfloat16)


def attention(request_of_slot, block_of_slot, qkv, pbuf, bucket, table):
    vmem, hbm = pl.BlockSpec(memory_space=pltpu.VMEM), pl.BlockSpec(memory_space=pl.ANY)
    smem = pl.BlockSpec(memory_space=pltpu.SMEM)
    return pl.pallas_call(
        attention_kernel,
        name="attention",
        out_shape=jax.ShapeDtypeStruct((SLOT, COLS), jnp.bfloat16),
        in_specs=[smem, smem, vmem, hbm, vmem, vmem],
        out_specs=vmem,
        scratch_shapes=[
            pltpu.SMEM((GROUPS * GROUP_BLOCKS,), jnp.int32),
            pltpu.VMEM((GROUP_BLOCKS, 2, PB, COLS), jnp.bfloat16),
            pltpu.VMEM((HEADS, PREFIX + DIST), jnp.float32),
            pltpu.VMEM((HEADS // 2, 5, 128, 256), jnp.float32),
            pltpu.SemaphoreType.DMA((GROUP_BLOCKS,)),
        ],
        compiler_params=pltpu.CompilerParams(vmem_limit_bytes=48 << 20),
    )(request_of_slot, block_of_slot, qkv, pbuf, bucket, table)


def body(
    hidden,
    norm_gain,
    qkv_weight,
    out_weight,
    bias_table,
    prefix_cache,
    suffix_lengths,
    request_of_slot,
    block_of_slot,
    bias_bucket,
):
    request = lax.dynamic_index_in_dim(request_of_slot, lax.axis_index("seq"), 0, keepdims=False)
    length = lax.dynamic_index_in_dim(suffix_lengths, request, 0, keepdims=False)
    qkv, pbuf = gather(hidden[0], norm_gain[None], qkv_weight.transpose(1, 0, 2), prefix_cache)
    attn = attention(
        request_of_slot, block_of_slot, qkv, pbuf.reshape(64, 2, PB, COLS), bias_bucket[None], bias_table.T
    )
    product = jnp.dot(attn, out_weight, preferred_element_type=jnp.float32)
    alive = jnp.arange(SLOT, dtype=jnp.int32) < length
    summed = lax.psum_scatter(
        jnp.where(alive[:, None], product, 0.0).astype(jnp.bfloat16),
        "tp",
        scatter_dimension=0,
        tiled=True,
    )
    return summed[None]


def solution(mesh):
    return jax.shard_map(
        body,
        mesh=mesh,
        in_specs=(
            P("seq", "tp", None),
            P(),
            P(None, None, "tp"),
            P("tp", None),
            P(None, "tp"),
            P("seq", None, "tp"),
            P(),
            P(),
            P(),
            P(),
        ),
        out_specs=P("seq", "tp", None),
        check_vma=False,
    )
```

```python
import functools

import jax
import jax.numpy as jnp
from jax import lax
from jax.experimental import pallas as pl
from jax.experimental.pallas import tpu as pltpu
from jax.sharding import PartitionSpec as P

MESH = pl.DeviceIdType.MESH
TP = 4
ROWS = 128
SLOT = ROWS * TP
D = 2048
COLS = 512
HEADS = 8
PB = 8
PREFIX = 128
CACHE = 512
DIST = 640
BUCKETS = 32
RG = 16
NEG = -1e30
CH = 4
CROWS = ROWS // CH


def aligned(start, unit):
    return pl.multiple_of(start, unit)


def remote(src, dst, send_sem, recv_sem, to):
    return pltpu.make_async_remote_copy(
        src_ref=src, dst_ref=dst, send_sem=send_sem, recv_sem=recv_sem, device_id=to, device_id_type=MESH
    )


class Track:
    def __init__(self, view, columns, off, unit, me, peers, send, recv):
        self.view, self.columns, self.off, self.unit = view, columns, off, unit
        self.me, self.peers, self.send, self.recv = me, peers, send, recv

    def region(self, stage, i, part=None):
        count = self.unit if stage == 0 else 4 * self.unit
        start = self.off + (self.me[1] * 4 * self.unit + i * self.unit if stage == 0 else i * 4 * self.unit)
        half = self.columns // 2
        columns = pl.ds(0, self.columns) if part is None else pl.ds(part * half, half)
        return self.view(pl.ds(aligned(start, self.unit), count), columns)

    def copy(self, stage, k, i):
        region = self.region(stage, i, None if k < 2 else k - 2)
        return remote(region, region, self.send.at[stage, k], self.recv.at[stage, k], self.peers[stage][k % 2])

    def near(self, stage):
        me = self.me[stage]
        return lax.rem(me + 3, 4), lax.rem(me + 1, 4), lax.rem(me + 2, 4)

    def first(self, stage):
        for k in range(2):
            self.copy(stage, k, self.me[stage]).start()

    def second(self, stage):
        behind, ahead, _ = self.near(stage)
        self.copy(stage, 0, behind).wait_recv()
        self.copy(stage, 1, ahead).wait_recv()
        self.copy(stage, 2, behind).start()
        self.copy(stage, 3, ahead).start()

    def complete(self, stage):
        far = self.near(stage)[2]
        self.copy(stage, 2, far).wait_recv()
        self.copy(stage, 3, far).wait_recv()

    def drain(self):
        for stage in range(2):
            behind, ahead, _ = self.near(stage)
            for k, i in enumerate((self.me[stage], self.me[stage], behind, ahead)):
                self.copy(stage, k, i).wait_send()


def kernel(
    request_ref, block_ref, length_ref, hid, gain_ref, w_hbm, pref, wo_hbm, bucket_ref, table_ref, out_ref,
    wbuf, hbuf, nbuf, acc, qkv, prefv, kvown, pbuf, tab, bias, tiles, wo, won, asend, aall,
    loc, own_s, sib_s, fwd_s, h_r, wz_s, wz_r, tb_s, tb_r, pz_s, pz_r, oz_s, oz_r,
    wt_s, wt_r, pt_s, pt_r, ot_s, ot_r, wc_s, wc_r, oc_s, oc_r, at_s, at_r,
):
    s = lax.axis_index("seq")
    t = lax.axis_index("tp")
    x, y, zh, c = s // 16, lax.rem(s // 4, 4), lax.rem(s // 2, 2), lax.rem(s, 2)
    side = t // 2
    leader = c == side
    inner = (t == 1) | (t == 2)
    beside = t + 1 - 2 * lax.rem(t, 2)
    across = lax.rem(t + 2, 4)
    group = lax.rem(t, 2) + 2 * c

    def at(zh_, c_, t_):
        return (((x * 4 + y) * 2 + zh_) * 2 + c_, t_)

    def column(x_, y_):
        return (((x_ * 4 + y_) * 2 + zh) * 2 + c, t)

    def along(step):
        other = lax.rem(zh * 4 + t + step + 8, 8)
        return at(other // 4, c, lax.rem(other, 4))

    xs = (column(lax.rem(x + 1, 4), y), column(lax.rem(x + 3, 4), y))
    ys = (column(x, lax.rem(y + 1, 4)), column(x, lax.rem(y + 3, 4)))
    core = at(zh, 1 - c, t)

    partners = [at(zh, lax.rem(c + dc, 2), lax.rem(t + dt, 4)) for dt in range(4) for dc in range(2) if dt or dc]
    partners += [at(1 - zh, c_, t_) for t_ in (t, across) for c_ in (c, 1 - c)]
    partners += [*xs, *ys]
    barrier = pltpu.get_barrier_semaphore()
    for partner in partners:
        pl.semaphore_signal(barrier, inc=1, device_id=partner, device_id_type=MESH)

    load_pref = pltpu.make_async_copy(pref, prefv, loc.at[0])
    load_pref.start()
    load_own = pltpu.make_async_copy(hid, hbuf.at[pl.ds(aligned(t * ROWS, ROWS), ROWS)], loc.at[1])

    @pl.when(leader)
    def _():
        load_own.start()

    load_w = pltpu.make_async_copy(w_hbm, wbuf.at[0], loc.at[2])
    load_w.start()
    load_wo = pltpu.make_async_copy(wo_hbm, won, loc.at[3])
    load_wo.start()
    load_pref.wait()
    both = prefv[...].astype(jnp.float32)
    kvown[0] = both[:, 0, :].astype(jnp.bfloat16)
    kvown[1] = both[:, 1, :].astype(jnp.bfloat16)
    pl.semaphore_wait(barrier, len(partners))

    def prefix_row(kv, zh_, c_):
        place = (y * 4 + x) if kv == 0 else (x * 4 + y)
        return pl.ds(aligned((place * 4 + zh_ * 2 + c_) * PB, PB), PB)

    def prefix_copy(target, kv, zh_, c_, to):
        rows = prefix_row(kv, zh_, c_)
        return remote(kvown.at[kv], pbuf.at[kv, rows], pz_s.at[target, kv], pz_r.at[zh_ * 2 + c_, kv], to)

    readers = (at(1 - zh, side, t), at(zh, side, across), at(1 - zh, side, across))
    own_prefix = [
        pltpu.make_async_copy(kvown.at[kv], pbuf.at[kv, prefix_row(kv, zh, c)], loc.at[4 + kv]) for kv in range(2)
    ]
    for kv in range(2):
        for k, reader in enumerate(readers):
            prefix_copy(k, kv, zh, c, reader).start()

        @pl.when(leader)
        def _():
            own_prefix[kv].start()

        @pl.when(jnp.logical_not(leader))
        def _():
            prefix_copy(3, kv, zh, c, core).start()

    send_table = remote(table_ref, tab, tb_s.at[0], tb_r.at[0], at(zh, c, across))
    send_table.start()

    def weight_row(hh):
        return hh * 1024 + c * 512 + ((y * 4 + x) if hh == 0 else (x * 4 + y)) * 32

    def weight_piece(hh):
        rows = pl.ds(aligned(weight_row(hh), 32), 32)
        return remote(
            w_hbm.at[:, rows], wbuf.at[1, :, rows], wz_s.at[hh], wz_r.at[hh], along(2 if hh == 0 else -2)
        )

    for hh in range(2):
        weight_piece(hh).start()

    def quarter(k):
        j = jnp.where(t < 2, 2, 1)
        f = jnp.where(t < 2, 3, 0)
        return (t, beside, j, f)[k]

    def chunk(q, j):
        return hbuf.at[pl.ds(aligned(q * ROWS + j * CROWS, CROWS), CROWS)]

    own_to = at(zh, c, jnp.where(leader, beside, quarter(2)))

    def own_copy(j):
        return remote(hid.at[pl.ds(j * CROWS, CROWS)], chunk(t, j), own_s.at[j], h_r.at[t, j], own_to)

    def sibling_copy(k, j):
        q = quarter(k)
        src = hid.at[pl.ds(j * CROWS, CROWS)] if k == 0 else chunk(q, j)
        return remote(src, chunk(q, j), sib_s.at[k, j], h_r.at[q, j], core)

    def forward_copy(k, j):
        q = quarter(k)
        return remote(chunk(q, j), chunk(q, j), fwd_s.at[k, j], h_r.at[q, j], at(zh, c, beside))

    for j in range(CH):
        own_copy(j).start()

    for j in range(CH):
        @pl.when(leader)
        def _():
            sibling_copy(0, j).start()

    def out_row(hh):
        return hh * 256 + c * 128 + ((y * 4 + x) if hh == 0 else (x * 4 + y)) * 8

    def out_piece(d, hh):
        rows = pl.ds(aligned(out_row(hh), 8), 8)
        return remote(
            wo_hbm.at[rows], wo.at[3 - d, rows], oz_s.at[d - 1, hh], oz_r.at[3 - d, hh], at(zh, c, lax.rem(t + d, 4))
        )

    def arrive(k, j):
        if k == 0:
            @pl.when(jnp.logical_not(leader))
            def _():
                sibling_copy(0, j).wait_recv()
        else:
            sibling_copy(k, j).wait_recv()

            @pl.when(leader)
            def _():
                sibling_copy(k, j).start()

            if k >= 2:
                @pl.when(leader & inner)
                def _():
                    forward_copy(k, j).start()

    def tracks(views, columns, offs, unit, send, recv):
        first = Track(views[0], columns, offs[0], unit, (x, y), (xs, ys), send.at[0], recv.at[0])
        other = Track(views[1], columns, offs[1], unit, (y, x), (ys, xs), send.at[1], recv.at[1])
        return first, other

    w_view = lambda rows, columns: wbuf.at[1, :, rows, columns]
    o_view = lambda rows, columns: wo.at[:, rows, columns]
    w_tracks = tracks((w_view, w_view), COLS, (c * 512, 1024 + c * 512), 32, wt_s, wt_r)
    p_tracks = tracks(
        (lambda rows, columns: pbuf.at[0, rows, columns], lambda rows, columns: pbuf.at[1, rows, columns]),
        COLS, (0, 0), 32, pt_s, pt_r,
    )
    o_tracks = tracks((o_view, o_view), D, (c * 128, 256 + c * 128), 8, ot_s, ot_r)

    def core_weights(hh, i, core_):
        start = hh * 1024 + core_ * 512 + i * 128
        region = wbuf.at[1, :, pl.ds(aligned(start, 128), 128)]
        return remote(region, region, wc_s.at[hh, i], wc_r.at[hh, i], core)

    def core_out(hh, core_):
        region = wo.at[:, pl.ds(aligned(hh * 256 + core_ * 128, 128), 128)]
        return remote(region, region, oc_s.at[hh], oc_r.at[hh], core)

    def each(which, action, stage):
        for track in which:
            getattr(track, action)(stage)

    def norm(k):
        rows = pl.ds(aligned(quarter(k) * ROWS, ROWS), ROWS)
        gain = jnp.concatenate([gain_ref[i : i + 1, :].astype(jnp.float32) for i in range(D // 128)], 1)
        states = hbuf[rows, :].astype(jnp.float32)
        scale = lax.rsqrt(jnp.mean(states * states, -1, keepdims=True) + 1e-06)
        nbuf[rows, :] = (states * scale * gain).astype(jnp.bfloat16)

    for kv in range(2):
        for zh_ in range(2):
            for c_ in range(2):
                mine = leader & (zh == zh_) & (c == c_)

                @pl.when(jnp.logical_not(mine))
                def _():
                    prefix_copy(0, kv, zh_, c_, core).wait_recv()

        @pl.when(leader)
        def _():
            own_prefix[kv].wait()

    each(p_tracks, "first", 0)
    send_table.wait_recv()

    for j in range(2):
        arrive(0, j)
        arrive(1, j)
    for hh in range(2):
        weight_piece(hh).wait_recv()
    each(w_tracks, "first", 0)
    each(p_tracks, "second", 0)
    for d in range(1, 4):
        for hh in range(2):
            out_piece(d, hh).start()
    each(w_tracks, "second", 0)
    for j in range(2, CH):
        arrive(0, j)
        arrive(1, j)
    each(w_tracks, "complete", 0)
    each(w_tracks, "first", 1)
    each(p_tracks, "complete", 0)
    each(p_tracks, "first", 1)

    bucket = jnp.concatenate([bucket_ref[i : i + 1, :] for i in range(DIST // 128)], 1)
    bucket = jnp.broadcast_to(bucket, (HEADS, DIST))
    table = jnp.where(leader, table_ref[...], tab[...])
    row = jnp.zeros((HEADS, DIST), jnp.float32)
    for b in range(BUCKETS):
        row = jnp.where(bucket == b, table[:, b : b + 1], row)
    bias[:, :PREFIX] = jnp.full((HEADS, PREFIX), NEG, jnp.float32)
    bias[:, PREFIX:] = row

    def build(h):
        for delta in range(5):
            window = jnp.broadcast_to(bias[h : h + 1, delta * 128 : delta * 128 + 256], (128, 256))
            rolled = pltpu.roll(window, 0, 1, stride=1, stride_axis=0)
            tiles[h // 2, delta, :, (h % 2) * 128 : (h % 2) * 128 + 128] = rolled[:, 128:]

    for j in range(CH):
        arrive(2, j)
        build(j)
    each(p_tracks, "second", 1)
    for rho in range(3):
        for hh in range(2):
            out_piece(3 - rho, hh).wait_recv()
    each(o_tracks, "first", 0)

    @pl.when(leader)
    def _():
        load_own.wait()

    norm(0)
    each(o_tracks, "second", 0)
    for j in range(CH):
        arrive(3, j)
        build(CH + j)
    norm(1)
    each(w_tracks, "second", 1)
    each(o_tracks, "complete", 0)

    @pl.when(leader)
    def _():
        for hh, me in ((0, y), (1, x)):
            for i in (me, lax.rem(me + 1, 4), lax.rem(me + 3, 4)):
                core_weights(hh, i, c).start()

    norm(2)
    norm(3)
    each(p_tracks, "complete", 1)
    each(w_tracks, "complete", 1)
    each(o_tracks, "first", 1)

    @pl.when(leader)
    def _():
        for hh, me in ((0, y), (1, x)):
            core_weights(hh, lax.rem(me + 2, 4), c).start()

    load_w.wait()
    which = jnp.where(leader, 0, 1)
    for step, (hh, core_) in enumerate(((0, c), (1, c), (0, 1 - c), (1, 1 - c))):
        if step >= 2:
            @pl.when(jnp.logical_not(leader))
            def _():
                for i in range(4):
                    core_weights(hh, i, core_).wait_recv()

        rows = pl.ds(aligned(hh * 1024 + core_ * 512, 512), 512)
        for i in range(3):
            columns = slice(i * COLS, (i + 1) * COLS)
            part = jnp.dot(nbuf[:, rows], wbuf[which, i, rows, :], preferred_element_type=jnp.float32)
            if step == 0:
                acc[:, columns] = part
            elif step < 3:
                acc[:, columns] += part
            else:
                qkv[:, columns] = (acc[:, columns] + part).astype(jnp.bfloat16)

    slot = ((x * 4 + y) * 2 + zh) * 2 + side
    first_row = request_ref[slot] // RG * PREFIX
    lane = lax.broadcasted_iota(jnp.int32, (1, CACHE), 1)
    chosen = []
    for kv in range(2):
        target = jnp.zeros((1, CACHE), jnp.int32)
        for place in range(CACHE // PB):
            owner = (place // 4 % 4 * 4 + place // 16) * 4 + place % 4 if kv == 0 else place
            target = jnp.where(lane // PB == place, block_ref[owner] * PB, target)
        target = target + lane % PB - first_row
        match = lax.broadcasted_iota(jnp.int32, (PREFIX, CACHE), 0) == jnp.broadcast_to(target, (PREFIX, CACHE))
        pick = jnp.where(match, 1.0, 0.0).astype(jnp.bfloat16)
        chosen.append(jnp.dot(pick, pbuf[kv], preferred_element_type=jnp.float32).astype(jnp.bfloat16))

    low = lax.broadcasted_iota(jnp.int32, (128, 128), 1) < 64
    keys, values = [], []
    for p in range(HEADS // 2):
        lanes = slice(p * 128, p * 128 + 128)
        keys.append(chosen[0][:, lanes])
        values.append(
            jnp.concatenate([chosen[1][:, lanes], qkv[:, 2 * COLS + p * 128 : 2 * COLS + p * 128 + 128]], 0).T
        )

    def attend(r):
        for p in range(HEADS // 2):
            lanes = slice(p * 128, p * 128 + 128)
            query = qkv[r * 128 : r * 128 + 128, lanes]
            zero = jnp.zeros_like(query)
            stacked = jnp.concatenate([jnp.where(low, query, zero), jnp.where(low, zero, query)], 0)
            blocks = []
            for kb in range(r + 2):
                key = keys[p] if kb == 0 else qkv[kb * 128 - 128 : kb * 128, COLS + p * 128 : COLS + p * 128 + 128]
                part = lax.dot_general(key, stacked, (((1,), (1,)), ((), ())), preferred_element_type=jnp.float32)
                blocks.append(part + tiles[p, r + 1 - kb])
            top = functools.reduce(jnp.maximum, [jnp.max(b, 0, keepdims=True) for b in blocks])
            probs = [jnp.exp(b - top) for b in blocks]
            denom = functools.reduce(jnp.add, [jnp.sum(b, 0, keepdims=True) for b in probs])
            probs = jnp.concatenate([b.astype(jnp.bfloat16) for b in probs], 0)
            out = jnp.dot(values[p][:, : (r + 2) * 128], probs, preferred_element_type=jnp.float32) / denom
            pair = jnp.concatenate([out[:64, :128], out[64:, 128:]], 0)
            asend[r, :, lanes] = pair.T.astype(jnp.bfloat16)

    def attn_copy(r):
        return remote(asend.at[r], aall.at[group], at_s.at[r], at_r.at[group], at(zh, side, r))

    own_attn = pltpu.make_async_copy(asend.at[t], aall.at[group], loc.at[6])

    for r in (3, 0, 2, 1):
        attend(r)
        stays = leader & (t == r)

        @pl.when(stays)
        def _():
            own_attn.start()

        @pl.when(jnp.logical_not(stays))
        def _():
            attn_copy(r).start()

        if r == 0:
            each(o_tracks, "second", 1)

    each(o_tracks, "complete", 1)
    for hh in range(2):
        core_out(hh, c).start()
    load_wo.wait()
    for hh in range(2):
        core_out(hh, 1 - c).wait_recv()

    def attn_arrived(g):
        remote(asend.at[0], aall.at[g], at_s.at[0], at_r.at[g], core).wait_recv()

    total = None
    for rho in range(-1, 3):
        g = lax.rem(t + 1 + rho, 4)
        if rho < 0:
            @pl.when(leader)
            def _():
                own_attn.wait()

            @pl.when(jnp.logical_not(leader))
            def _():
                attn_arrived(g)
        else:
            attn_arrived(g)
        weights = won[...] if rho < 0 else wo[rho]
        part = jnp.dot(aall[g], weights, preferred_element_type=jnp.float32)
        total = part if total is None else total + part
    length = length_ref[request_ref[s]]
    position = t * ROWS + lax.broadcasted_iota(jnp.int32, (ROWS, D), 0)
    out_ref[...] = jnp.where(position < length, total, 0.0).astype(jnp.bfloat16)

    for kv in range(2):
        for k, reader in enumerate(readers):
            prefix_copy(k, kv, zh, c, reader).wait_send()

        @pl.when(jnp.logical_not(leader))
        def _():
            prefix_copy(3, kv, zh, c, core).wait_send()

    send_table.wait_send()
    for hh in range(2):
        weight_piece(hh).wait_send()
        core_out(hh, c).wait_send()
        for d in range(1, 4):
            out_piece(d, hh).wait_send()
    for j in range(CH):
        own_copy(j).wait_send()

    @pl.when(leader)
    def _():
        for j in range(CH):
            for k in range(4):
                sibling_copy(k, j).wait_send()
        for hh in range(2):
            for i in range(4):
                core_weights(hh, i, c).wait_send()

    @pl.when(leader & inner)
    def _():
        for j in range(CH):
            for k in range(2, 4):
                forward_copy(k, j).wait_send()

    for track in (*w_tracks, *p_tracks, *o_tracks):
        track.drain()
    for r in range(TP):
        @pl.when(jnp.logical_not(leader & (t == r)))
        def _():
            attn_copy(r).wait_send()


def body(
    hidden,
    norm_gain,
    qkv_weight,
    out_weight,
    bias_table,
    prefix_cache,
    suffix_lengths,
    request_of_slot,
    block_of_slot,
    bias_bucket,
):
    vmem, smem = pl.BlockSpec(memory_space=pltpu.VMEM), pl.BlockSpec(memory_space=pltpu.SMEM)
    hbm = pl.BlockSpec(memory_space=pltpu.HBM)
    dma = pltpu.SemaphoreType.DMA
    bf16, f32 = jnp.bfloat16, jnp.float32
    out = pl.pallas_call(
        kernel,
        name="sublayer",
        out_shape=jax.ShapeDtypeStruct((ROWS, D), bf16),
        in_specs=[smem, smem, smem, hbm, vmem, hbm, hbm, hbm, vmem, vmem],
        out_specs=vmem,
        scratch_shapes=[
            pltpu.VMEM((2, 3, D, COLS), bf16),
            pltpu.VMEM((SLOT, D), bf16),
            pltpu.VMEM((SLOT, D), bf16),
            pltpu.VMEM((SLOT, 3 * COLS), f32),
            pltpu.VMEM((SLOT, 3 * COLS), bf16),
            pltpu.VMEM((PB, 2, COLS), bf16),
            pltpu.VMEM((2, PB, COLS), bf16),
            pltpu.VMEM((2, CACHE, COLS), bf16),
            pltpu.VMEM((HEADS, BUCKETS), f32),
            pltpu.VMEM((HEADS, PREFIX + DIST), f32),
            pltpu.VMEM((HEADS // 2, 5, 128, 256), f32),
            pltpu.VMEM((3, COLS, D), bf16),
            pltpu.VMEM((COLS, D), bf16),
            pltpu.VMEM((TP, ROWS, COLS), bf16),
            pltpu.VMEM((TP, ROWS, COLS), bf16),
            dma((7,)), dma((CH,)), dma((4, CH)), dma((4, CH)), dma((4, CH)),
            dma((2,)), dma((2,)), dma((1,)), dma((1,)), dma((4, 2)), dma((4, 2)), dma((3, 2)), dma((3, 2)),
            dma((2, 2, 4)), dma((2, 2, 4)), dma((2, 2, 4)), dma((2, 2, 4)), dma((2, 2, 4)), dma((2, 2, 4)),
            dma((2, 4)), dma((2, 4)), dma((2,)), dma((2,)), dma((4,)), dma((4,)),
        ],
        compiler_params=pltpu.CompilerParams(collective_id=0, has_side_effects=True, vmem_limit_bytes=60 << 20),
    )(
        request_of_slot,
        block_of_slot,
        suffix_lengths,
        hidden[0],
        norm_gain.reshape(D // 128, 128),
        qkv_weight.transpose(1, 0, 2),
        prefix_cache,
        out_weight,
        bias_bucket.reshape(DIST // 128, 128),
        bias_table.T,
    )
    return out[None]


def solution(mesh):
    return jax.shard_map(
        body,
        mesh=mesh,
        in_specs=(
            P("seq", "tp", None),
            P(),
            P(None, None, "tp"),
            P("tp", None),
            P(None, "tp"),
            P("seq", None, "tp"),
            P(),
            P(),
            P(),
            P(),
        ),
        out_specs=P("seq", "tp", None),
        check_vma=False,
    )
```

```python
import functools

import jax
import jax.numpy as jnp
from jax import lax
from jax.experimental import pallas as pl
from jax.experimental.pallas import tpu as pltpu
from jax.sharding import PartitionSpec as P

MESH = pl.DeviceIdType.MESH
TP = 4
ROWS = 128
SLOT = ROWS * TP
D = 2048
COLS = 512
HEADS = 8
PB = 8
PREFIX = 128
CACHE = 512
DIST = 640
BUCKETS = 32
RG = 16
NEG = -1e30
CH = 4
CROWS = ROWS // CH


def aligned(start, unit):
    return pl.multiple_of(start, unit)


def remote(src, dst, send_sem, recv_sem, to):
    return pltpu.make_async_remote_copy(
        src_ref=src, dst_ref=dst, send_sem=send_sem, recv_sem=recv_sem, device_id=to, device_id_type=MESH
    )


class Track:
    def __init__(self, view, columns, off, unit, step, me, peers, send, recv):
        self.view, self.columns, self.off, self.unit, self.step = view, columns, off, unit, step
        self.me, self.peers, self.send, self.recv = me, peers, send, recv

    def region(self, stage, i, part=None):
        count = self.unit if stage == 0 else 4 * self.unit
        start = self.off + (self.me[1] * self.step + i * self.unit if stage == 0 else i * self.step)
        half = self.columns // 2
        columns = pl.ds(0, self.columns) if part is None else pl.ds(part * half, half)
        return self.view(pl.ds(aligned(start, self.unit), count), columns)

    def near(self, stage, k, part, i):
        region = self.region(stage, i, part)
        index = k * 2 + part
        return remote(region, region, self.send.at[stage, index], self.recv.at[stage, index], self.peers[stage][k])

    def far(self, stage, k, i):
        region = self.region(stage, i, k)
        return remote(region, region, self.send.at[stage, 4 + k], self.recv.at[stage, 4 + k], self.peers[stage][k])

    def around(self, stage):
        me = self.me[stage]
        return lax.rem(me + 3, 4), lax.rem(me + 1, 4), lax.rem(me + 2, 4)

    def first(self, stage):
        for k, part in ((0, 0), (1, 1), (0, 1), (1, 0)):
            self.near(stage, k, part, self.me[stage]).start()

    def second(self, stage):
        behind, ahead, _ = self.around(stage)
        for k, i in enumerate((behind, ahead)):
            self.near(stage, k, k, i).wait_recv()
            self.far(stage, k, i).start()

    def rest(self, stage):
        behind, ahead, _ = self.around(stage)
        for k, i in enumerate((behind, ahead)):
            self.near(stage, k, 1 - k, i).wait_recv()

    def complete(self, stage):
        opposite = self.around(stage)[2]
        for k in range(2):
            self.far(stage, k, opposite).wait_recv()

    def drain(self, stages=(0, 1)):
        for stage in stages:
            behind, ahead, _ = self.around(stage)
            for k, i in enumerate((behind, ahead)):
                for part in range(2):
                    self.near(stage, k, part, self.me[stage]).wait_send()
                self.far(stage, k, i).wait_send()


def kernel(
    request_ref, block_ref, length_ref, hid, gain_ref, w_hbm, pref, wo_hbm, bucket_ref, table_ref, out_ref,
    wbuf, hbuf, nbuf, acc, qkv, prefv, kvown, pbuf, tab, bias, tiles, wo, won, asend, aall,
    loc, own_s, sib_s, fwd_s, h_r, wz_s, wz_r, tb_s, tb_r, pz_s, pz_r, oz_s, oz_r,
    wt_s, wt_r, pt_s, pt_r, ot_s, ot_r, wn_s, wn_r, wf_s, wf_r, wb_s, wb_r, oc_s, oc_r, at_s, at_r,
):
    s = lax.axis_index("seq")
    t = lax.axis_index("tp")
    x, y, zh, c = s // 16, lax.rem(s // 4, 4), lax.rem(s // 2, 2), lax.rem(s, 2)
    side = t // 2
    leader = c == side
    inner = (t == 1) | (t == 2)
    beside = t + 1 - 2 * lax.rem(t, 2)
    across = lax.rem(t + 2, 4)
    group = lax.rem(t, 2) + 2 * c

    def at(zh_, c_, t_):
        return (((x * 4 + y) * 2 + zh_) * 2 + c_, t_)

    def column(x_, y_, c_):
        return (((x_ * 4 + y_) * 2 + zh) * 2 + c_, t)

    def along(step):
        other = lax.rem(zh * 4 + t + step + 8, 8)
        return at(other // 4, c, lax.rem(other, 4))

    x1, x3, y1, y3 = lax.rem(x + 1, 4), lax.rem(x + 3, 4), lax.rem(y + 1, 4), lax.rem(y + 3, 4)
    foreign = 1 - side
    xs, xf = [(column(x1, y, c_), column(x3, y, c_)) for c_ in (c, foreign)]
    ys, yf = [(column(x, y1, c_), column(x, y3, c_)) for c_ in (c, foreign)]
    core = at(zh, 1 - c, t)

    partners = [at(zh, lax.rem(c + dc, 2), lax.rem(t + dt, 4)) for dt in range(4) for dc in range(2) if dt or dc]
    partners += [at(1 - zh, c_, t_) for t_ in (t, across) for c_ in (c, 1 - c)]
    partners += [at(1 - zh, c, 3 - t)]
    partners += [
        (((x_ * 4 + y_) * 2 + zh) * 2 + c_, t)
        for x_, y_ in ((x1, y), (x3, y), (x, y1), (x, y3))
        for c_ in (c, 1 - c)
    ]
    barrier = pltpu.get_barrier_semaphore()
    for partner in partners:
        pl.semaphore_signal(barrier, inc=1, device_id=partner, device_id_type=MESH)

    load_pref = pltpu.make_async_copy(pref, prefv, loc.at[0])
    load_pref.start()
    load_own = pltpu.make_async_copy(hid, hbuf.at[pl.ds(aligned(t * ROWS, ROWS), ROWS)], loc.at[1])

    @pl.when(leader)
    def _():
        load_own.start()

    load_w = pltpu.make_async_copy(w_hbm, wbuf.at[0], loc.at[2])
    load_w.start()
    load_wo = pltpu.make_async_copy(wo_hbm, won, loc.at[3])
    load_wo.start()
    load_pref.wait()
    both = prefv[...].astype(jnp.float32)
    kvown[0] = both[:, 0, :].astype(jnp.bfloat16)
    kvown[1] = both[:, 1, :].astype(jnp.bfloat16)
    pl.semaphore_wait(barrier, len(partners))

    def weight_row(hh):
        return hh * 1024 + c * 128 + ((y * 256 + x * 32) if hh == 0 else (x * 256 + y * 32))

    def weight_piece(hh):
        rows = pl.ds(aligned(weight_row(hh), 32), 32)
        return remote(
            w_hbm.at[:, rows], wbuf.at[1, :, rows], wz_s.at[hh], wz_r.at[hh], along(2 if hh == 0 else -2)
        )

    def prefix_row(kv, zh_, c_):
        place = (y * 4 + x) if kv == 0 else (x * 4 + y)
        return pl.ds(aligned((place * 4 + zh_ * 2 + c_) * PB, PB), PB)

    def prefix_copy(target, kv, zh_, c_, to):
        rows = prefix_row(kv, zh_, c_)
        return remote(kvown.at[kv], pbuf.at[kv, rows], pz_s.at[target, kv], pz_r.at[zh_ * 2 + c_, kv], to)

    readers = (at(1 - zh, side, t), at(zh, side, across), at(1 - zh, side, across))
    own_prefix = [
        pltpu.make_async_copy(kvown.at[kv], pbuf.at[kv, prefix_row(kv, zh, c)], loc.at[4 + kv]) for kv in range(2)
    ]
    for kv in range(2):
        for k, reader in enumerate(readers):
            prefix_copy(k, kv, zh, c, reader).start()

        @pl.when(leader)
        def _():
            own_prefix[kv].start()

        @pl.when(jnp.logical_not(leader))
        def _():
            prefix_copy(3, kv, zh, c, core).start()

    send_table = remote(table_ref, tab, tb_s.at[0], tb_r.at[0], at(zh, c, across))
    send_table.start()
    for hh in range(2):
        weight_piece(hh).start()

    def quarter(k):
        j = jnp.where(t < 2, 2, 1)
        f = jnp.where(t < 2, 3, 0)
        return (t, beside, j, f)[k]

    def chunk(q, j):
        return hbuf.at[pl.ds(aligned(q * ROWS + j * CROWS, CROWS), CROWS)]

    own_to = at(zh, c, jnp.where(leader, beside, quarter(2)))

    def own_copy(j):
        return remote(hid.at[pl.ds(j * CROWS, CROWS)], chunk(t, j), own_s.at[j], h_r.at[t, j], own_to)

    def sibling_copy(k, j):
        q = quarter(k)
        src = hid.at[pl.ds(j * CROWS, CROWS)] if k == 0 else chunk(q, j)
        return remote(src, chunk(q, j), sib_s.at[k, j], h_r.at[q, j], core)

    def forward_copy(k, j):
        q = quarter(k)
        return remote(chunk(q, j), chunk(q, j), fwd_s.at[k, j], h_r.at[q, j], at(zh, c, beside))

    for j in range(CH):
        @pl.when(leader)
        def _():
            sibling_copy(0, j).start()

    def out_row(hh):
        return hh * 256 + c * 128 + ((y * 4 + x) if hh == 0 else (x * 4 + y)) * 8

    def out_piece(d, hh):
        rows = pl.ds(aligned(out_row(hh), 8), 8)
        step = (1, (2, -2)[hh], -1)[d - 1]
        return remote(wo_hbm.at[rows], wo.at[3 - d, rows], oz_s.at[d - 1, hh], oz_r.at[3 - d, hh], along(step))

    def arrive(k, j):
        if k == 0:
            @pl.when(jnp.logical_not(leader))
            def _():
                sibling_copy(0, j).wait_recv()
        else:
            sibling_copy(k, j).wait_recv()

            @pl.when(leader)
            def _():
                sibling_copy(k, j).start()

            if k >= 2:
                @pl.when(leader & inner)
                def _():
                    forward_copy(k, j).start()

    def tracks(views, columns, offs, unit, step, send, recv):
        first = Track(views[0], columns, offs[0], unit, step, (x, y), (xs, ys), send.at[0], recv.at[0])
        other = Track(views[1], columns, offs[1], unit, step, (y, x), (ys, xs), send.at[1], recv.at[1])
        return first, other

    w_view = lambda rows, columns: wbuf.at[1, :, rows, columns]
    o_view = lambda rows, columns: wo.at[:, rows, columns]
    w_tracks = tracks((w_view, w_view), COLS, (c * 128, 1024 + c * 128), 32, 256, wt_s, wt_r)
    p_tracks = tracks(
        (lambda rows, columns: pbuf.at[0, rows, columns], lambda rows, columns: pbuf.at[1, rows, columns]),
        COLS, (0, 0), 32, 128, pt_s, pt_r,
    )
    o_tracks = tracks((o_view, o_view), D, (c * 128, 256 + c * 128), 8, 32, ot_s, ot_r)

    places = ((y, y3, y1, yf), (x, x3, x1, xf))

    def w_region(hh, core_, i, part=None):
        rows = pl.ds(aligned(hh * 1024 + i * 256 + core_ * 128, 128), 128)
        half = COLS // 2
        return wbuf.at[1, :, rows, pl.ds(0, COLS) if part is None else pl.ds(part * half, half)]

    def w_near(hh, k, part, core_, i):
        region = w_region(hh, core_, i, part)
        return remote(region, region, wn_s.at[hh, k, part], wn_r.at[hh, core_, k, part], places[hh][3][k])

    def w_far(hh, k, core_, i):
        region = w_region(hh, core_, i, k)
        return remote(region, region, wf_s.at[hh, core_, k], wf_r.at[hh, core_, k], places[hh][3][k])

    def w_beside(hh, core_):
        region = w_region(hh, core_, places[hh][0])
        return remote(region, region, wb_s.at[hh], wb_r.at[hh], core)

    def w_first():
        for k, part in ((0, 0), (1, 1), (0, 1), (1, 0)):
            for hh in range(2):
                w_near(hh, k, part, c, places[hh][0]).start()

        @pl.when(leader)
        def _():
            for hh in range(2):
                w_beside(hh, c).start()

    def w_second():
        @pl.when(jnp.logical_not(leader))
        def _():
            for k in range(2):
                for hh in range(2):
                    for core_ in range(2):
                        w_near(hh, k, k, core_, places[hh][1 + k]).wait_recv()
                        w_far(hh, k, core_, places[hh][1 + k]).start()

    def w_rest():
        @pl.when(jnp.logical_not(leader))
        def _():
            for hh in range(2):
                w_beside(hh, 1 - c).wait_recv()
                for k in range(2):
                    for core_ in range(2):
                        w_near(hh, k, 1 - k, core_, places[hh][1 + k]).wait_recv()

    def w_complete():
        @pl.when(jnp.logical_not(leader))
        def _():
            for hh in range(2):
                for k in range(2):
                    for core_ in range(2):
                        w_far(hh, k, core_, lax.rem(places[hh][0] + 2, 4)).wait_recv()

    def core_out(hh, core_, i):
        region = wo.at[:, pl.ds(aligned(hh * 256 + core_ * 128 + i * 32, 32), 32)]
        return remote(region, region, oc_s.at[hh, i], oc_r.at[hh, i], core)

    def each(which, action, stage):
        for track in which:
            getattr(track, action)(stage)

    def norm(k):
        rows = pl.ds(aligned(quarter(k) * ROWS, ROWS), ROWS)
        gain = jnp.concatenate([gain_ref[i : i + 1, :].astype(jnp.float32) for i in range(D // 128)], 1)
        states = hbuf[rows, :].astype(jnp.float32)
        scale = lax.rsqrt(jnp.mean(states * states, -1, keepdims=True) + 1e-06)
        nbuf[rows, :] = (states * scale * gain).astype(jnp.bfloat16)

    def build_bias():
        bucket = jnp.concatenate([bucket_ref[i : i + 1, :] for i in range(DIST // 128)], 1)
        bucket = jnp.broadcast_to(bucket, (HEADS, DIST))
        table = jnp.where(leader, table_ref[...], tab[...])
        row = jnp.zeros((HEADS, DIST), jnp.float32)
        for b in range(BUCKETS):
            row = jnp.where(bucket == b, table[:, b : b + 1], row)
        bias[:, :PREFIX] = jnp.full((HEADS, PREFIX), NEG, jnp.float32)
        bias[:, PREFIX:] = row

    def build(h):
        for delta in range(5):
            window = jnp.broadcast_to(bias[h : h + 1, delta * 128 : delta * 128 + 256], (128, 256))
            rolled = pltpu.roll(window, 0, 1, stride=1, stride_axis=0)
            tiles[h // 2, delta, :, (h % 2) * 128 : (h % 2) * 128 + 128] = rolled[:, 128:]

    def prefix_arrived():
        for kv in range(2):
            for zh_ in range(2):
                for c_ in range(2):
                    mine = leader & (zh == zh_) & (c == c_)

                    @pl.when(jnp.logical_not(mine))
                    def _():
                        prefix_copy(0, kv, zh_, c_, core).wait_recv()

            @pl.when(leader)
            def _():
                own_prefix[kv].wait()

    prefix_arrived()
    each(p_tracks, "first", 0)
    send_table.wait_recv()
    build_bias()
    for hh in range(2):
        weight_piece(hh).wait_recv()
    each(w_tracks, "first", 0)
    for j in range(CH):
        own_copy(j).start()
    for d in range(1, 4):
        for hh in range(2):
            out_piece(d, hh).start()
    each(p_tracks, "second", 0)
    each(p_tracks, "rest", 0)
    each(p_tracks, "complete", 0)
    each(p_tracks, "first", 1)
    for h in range(3):
        build(h)
    each(w_tracks, "second", 0)
    each(w_tracks, "rest", 0)
    for j in range(CH):
        arrive(0, j)
    each(p_tracks, "second", 1)
    arrive(1, 0)
    arrive(2, 0)
    each(w_tracks, "complete", 0)
    w_first()
    for j in range(1, CH):
        arrive(1, j)
        arrive(2, j)

    @pl.when(leader)
    def _():
        load_own.wait()

    norm(0)
    for j in range(CH):
        arrive(3, j)
    w_second()
    for rho in range(3):
        for hh in range(2):
            out_piece(3 - rho, hh).wait_recv()
    each(o_tracks, "first", 0)
    norm(1)
    for h in range(3, HEADS):
        build(h)
    each(p_tracks, "rest", 1)
    each(p_tracks, "complete", 1)
    each(o_tracks, "second", 0)
    norm(2)
    norm(3)
    w_rest()
    load_w.wait()
    which = jnp.where(leader, 0, 1)

    def product(i, slices):
        total = None
        for hh, place in slices:
            rows = pl.ds(aligned(hh * 1024 + place * 256, 256), 256)
            part = jnp.dot(nbuf[:, rows], wbuf[which, i, rows, :], preferred_element_type=jnp.float32)
            total = part if total is None else total + part
        return total

    for i in range(3):
        acc[:, i * COLS : (i + 1) * COLS] = product(i, [(hh, places[hh][k]) for hh in range(2) for k in range(3)])
        if i == 0:
            each(o_tracks, "rest", 0)
            each(o_tracks, "complete", 0)
            each(o_tracks, "first", 1)
            for hh in range(2):
                core_out(hh, c, places[hh][0]).start()
    w_complete()
    for i in range(3):
        columns = slice(i * COLS, (i + 1) * COLS)
        far = product(i, [(hh, lax.rem(places[hh][0] + 2, 4)) for hh in range(2)])
        qkv[:, columns] = (acc[:, columns] + far).astype(jnp.bfloat16)

    slot = ((x * 4 + y) * 2 + zh) * 2 + side
    first_row = request_ref[slot] // RG * PREFIX
    lane = lax.broadcasted_iota(jnp.int32, (1, CACHE), 1)
    chosen = []
    for kv in range(2):
        target = jnp.zeros((1, CACHE), jnp.int32)
        for place in range(CACHE // PB):
            owner = (place // 4 % 4 * 4 + place // 16) * 4 + place % 4 if kv == 0 else place
            target = jnp.where(lane // PB == place, block_ref[owner] * PB, target)
        target = target + lane % PB - first_row
        match = lax.broadcasted_iota(jnp.int32, (PREFIX, CACHE), 0) == jnp.broadcast_to(target, (PREFIX, CACHE))
        pick = jnp.where(match, 1.0, 0.0).astype(jnp.bfloat16)
        chosen.append(jnp.dot(pick, pbuf[kv], preferred_element_type=jnp.float32).astype(jnp.bfloat16))

    low = lax.broadcasted_iota(jnp.int32, (128, 128), 1) < 64
    keys, values = [], []
    for p in range(HEADS // 2):
        lanes = slice(p * 128, p * 128 + 128)
        keys.append(chosen[0][:, lanes])
        values.append(
            jnp.concatenate([chosen[1][:, lanes], qkv[:, 2 * COLS + p * 128 : 2 * COLS + p * 128 + 128]], 0).T
        )

    def attend(r):
        for p in range(HEADS // 2):
            lanes = slice(p * 128, p * 128 + 128)
            query = qkv[r * 128 : r * 128 + 128, lanes]
            zero = jnp.zeros_like(query)
            stacked = jnp.concatenate([jnp.where(low, query, zero), jnp.where(low, zero, query)], 0)
            blocks = []
            for kb in range(r + 2):
                key = keys[p] if kb == 0 else qkv[kb * 128 - 128 : kb * 128, COLS + p * 128 : COLS + p * 128 + 128]
                part = lax.dot_general(key, stacked, (((1,), (1,)), ((), ())), preferred_element_type=jnp.float32)
                blocks.append(part + tiles[p, r + 1 - kb])
            top = functools.reduce(jnp.maximum, [jnp.max(b, 0, keepdims=True) for b in blocks])
            probs = [jnp.exp(b - top) for b in blocks]
            denom = functools.reduce(jnp.add, [jnp.sum(b, 0, keepdims=True) for b in probs])
            probs = jnp.concatenate([b.astype(jnp.bfloat16) for b in probs], 0)
            out = jnp.dot(values[p][:, : (r + 2) * 128], probs, preferred_element_type=jnp.float32) / denom
            pair = jnp.concatenate([out[:64, :128], out[64:, 128:]], 0)
            asend[r, :, lanes] = pair.T.astype(jnp.bfloat16)

    def attn_copy(r):
        return remote(asend.at[r], aall.at[group], at_s.at[r], at_r.at[group], at(zh, side, r))

    own_attn = pltpu.make_async_copy(asend.at[t], aall.at[group], loc.at[6])

    for r in (3, 0, 2, 1):
        attend(r)
        stays = leader & (t == r)

        @pl.when(stays)
        def _():
            own_attn.start()

        @pl.when(jnp.logical_not(stays))
        def _():
            attn_copy(r).start()

        if r == 3:
            each(o_tracks, "second", 1)
        if r == 2:
            each(o_tracks, "rest", 1)
            for hh in range(2):
                for k in range(2):
                    core_out(hh, c, places[hh][1 + k]).start()

    each(o_tracks, "complete", 1)
    for hh in range(2):
        core_out(hh, c, lax.rem(places[hh][0] + 2, 4)).start()
    load_wo.wait()
    for hh in range(2):
        for i in range(4):
            core_out(hh, 1 - c, i).wait_recv()

    def attn_arrived(g):
        remote(asend.at[0], aall.at[g], at_s.at[0], at_r.at[g], core).wait_recv()

    total = None
    for rho in range(-1, 3):
        g = lax.rem(t + 1 + rho, 4)
        if rho < 0:
            @pl.when(leader)
            def _():
                own_attn.wait()

            @pl.when(jnp.logical_not(leader))
            def _():
                attn_arrived(g)
        else:
            attn_arrived(g)
        weights = won[...] if rho < 0 else wo[rho]
        part = jnp.dot(aall[g], weights, preferred_element_type=jnp.float32)
        total = part if total is None else total + part
    length = length_ref[request_ref[s]]
    position = t * ROWS + lax.broadcasted_iota(jnp.int32, (ROWS, D), 0)
    out_ref[...] = jnp.where(position < length, total, 0.0).astype(jnp.bfloat16)

    for kv in range(2):
        for k, reader in enumerate(readers):
            prefix_copy(k, kv, zh, c, reader).wait_send()

        @pl.when(jnp.logical_not(leader))
        def _():
            prefix_copy(3, kv, zh, c, core).wait_send()

    send_table.wait_send()
    for hh in range(2):
        weight_piece(hh).wait_send()
        for i in range(4):
            core_out(hh, c, i).wait_send()
        for d in range(1, 4):
            out_piece(d, hh).wait_send()
        for k in range(2):
            for part in range(2):
                w_near(hh, k, part, c, places[hh][0]).wait_send()
    for j in range(CH):
        own_copy(j).wait_send()

    @pl.when(leader)
    def _():
        for j in range(CH):
            for k in range(4):
                sibling_copy(k, j).wait_send()
        for hh in range(2):
            w_beside(hh, c).wait_send()

    @pl.when(jnp.logical_not(leader))
    def _():
        for hh in range(2):
            for k in range(2):
                for core_ in range(2):
                    w_far(hh, k, core_, places[hh][1 + k]).wait_send()

    @pl.when(leader & inner)
    def _():
        for j in range(CH):
            for k in range(2, 4):
                forward_copy(k, j).wait_send()

    for track in w_tracks:
        track.drain((0,))
    for track in (*p_tracks, *o_tracks):
        track.drain()
    for r in range(TP):
        @pl.when(jnp.logical_not(leader & (t == r)))
        def _():
            attn_copy(r).wait_send()


def body(
    hidden,
    norm_gain,
    qkv_weight,
    out_weight,
    bias_table,
    prefix_cache,
    suffix_lengths,
    request_of_slot,
    block_of_slot,
    bias_bucket,
):
    vmem, smem = pl.BlockSpec(memory_space=pltpu.VMEM), pl.BlockSpec(memory_space=pltpu.SMEM)
    hbm = pl.BlockSpec(memory_space=pltpu.HBM)
    dma = pltpu.SemaphoreType.DMA
    bf16, f32 = jnp.bfloat16, jnp.float32
    out = pl.pallas_call(
        kernel,
        name="sublayer",
        out_shape=jax.ShapeDtypeStruct((ROWS, D), bf16),
        in_specs=[smem, smem, smem, hbm, vmem, hbm, hbm, hbm, vmem, vmem],
        out_specs=vmem,
        scratch_shapes=[
            pltpu.VMEM((2, 3, D, COLS), bf16),
            pltpu.VMEM((SLOT, D), bf16),
            pltpu.VMEM((SLOT, D), bf16),
            pltpu.VMEM((SLOT, 3 * COLS), f32),
            pltpu.VMEM((SLOT, 3 * COLS), bf16),
            pltpu.VMEM((PB, 2, COLS), bf16),
            pltpu.VMEM((2, PB, COLS), bf16),
            pltpu.VMEM((2, CACHE, COLS), bf16),
            pltpu.VMEM((HEADS, BUCKETS), f32),
            pltpu.VMEM((HEADS, PREFIX + DIST), f32),
            pltpu.VMEM((HEADS // 2, 5, 128, 256), f32),
            pltpu.VMEM((3, COLS, D), bf16),
            pltpu.VMEM((COLS, D), bf16),
            pltpu.VMEM((TP, ROWS, COLS), bf16),
            pltpu.VMEM((TP, ROWS, COLS), bf16),
            dma((7,)), dma((CH,)), dma((4, CH)), dma((4, CH)), dma((4, CH)),
            dma((2,)), dma((2,)), dma((1,)), dma((1,)), dma((4, 2)), dma((4, 2)), dma((3, 2)), dma((3, 2)),
            dma((2, 2, 6)), dma((2, 2, 6)), dma((2, 2, 6)), dma((2, 2, 6)), dma((2, 2, 6)), dma((2, 2, 6)),
            dma((2, 2, 2)), dma((2, 2, 2, 2)), dma((2, 2, 2)), dma((2, 2, 2)), dma((2,)), dma((2,)),
            dma((2, 4)), dma((2, 4)), dma((4,)), dma((4,)),
        ],
        compiler_params=pltpu.CompilerParams(collective_id=0, has_side_effects=True, vmem_limit_bytes=60 << 20),
    )(
        request_of_slot,
        block_of_slot,
        suffix_lengths,
        hidden[0],
        norm_gain.reshape(D // 128, 128),
        qkv_weight.transpose(1, 0, 2),
        prefix_cache,
        out_weight,
        bias_bucket.reshape(DIST // 128, 128),
        bias_table.T,
    )
    return out[None]


def solution(mesh):
    return jax.shard_map(
        body,
        mesh=mesh,
        in_specs=(
            P("seq", "tp", None),
            P(),
            P(None, None, "tp"),
            P("tp", None),
            P(None, "tp"),
            P("seq", None, "tp"),
            P(),
            P(),
            P(),
            P(),
        ),
        out_specs=P("seq", "tp", None),
        check_vma=False,
    )
```

```python
import functools

import jax
import jax.numpy as jnp
from jax import lax
from jax.experimental import pallas as pl
from jax.experimental.pallas import tpu as pltpu
from jax.sharding import PartitionSpec as P

MESH = pl.DeviceIdType.MESH
TP = 4
ROWS = 128
SLOT = ROWS * TP
D = 2048
COLS = 512
HEADS = 8
PB = 8
PREFIX = 128
CACHE = 512
DIST = 640
BUCKETS = 32
RG = 16
NEG = -1e30
CH = 4
CROWS = ROWS // CH


def aligned(start, unit):
    return pl.multiple_of(start, unit)


def remote(src, dst, send_sem, recv_sem, to):
    return pltpu.make_async_remote_copy(
        src_ref=src, dst_ref=dst, send_sem=send_sem, recv_sem=recv_sem, device_id=to, device_id_type=MESH
    )


class Track:
    def __init__(self, view, columns, off, unit, step, me, peers, send, recv):
        self.view, self.columns, self.off, self.unit, self.step = view, columns, off, unit, step
        self.me, self.peers, self.send, self.recv = me, peers, send, recv

    def region(self, stage, i, part=None):
        count = self.unit if stage == 0 else 4 * self.unit
        start = self.off + (self.me[1] * self.step + i * self.unit if stage == 0 else i * self.step)
        half = self.columns // 2
        columns = pl.ds(0, self.columns) if part is None else pl.ds(part * half, half)
        return self.view(pl.ds(aligned(start, self.unit), count), columns)

    def near(self, stage, k, part, i):
        region = self.region(stage, i, part)
        index = k * 2 + part
        return remote(region, region, self.send.at[stage, index], self.recv.at[stage, index], self.peers[stage][k])

    def far(self, stage, k, i):
        region = self.region(stage, i, k)
        return remote(region, region, self.send.at[stage, 4 + k], self.recv.at[stage, 4 + k], self.peers[stage][k])

    def around(self, stage):
        me = self.me[stage]
        return lax.rem(me + 3, 4), lax.rem(me + 1, 4), lax.rem(me + 2, 4)

    def first(self, stage):
        for k, part in ((0, 0), (1, 1), (0, 1), (1, 0)):
            self.near(stage, k, part, self.me[stage]).start()

    def second(self, stage):
        behind, ahead, _ = self.around(stage)
        for k, i in enumerate((behind, ahead)):
            self.near(stage, k, k, i).wait_recv()
            self.far(stage, k, i).start()

    def rest(self, stage):
        behind, ahead, _ = self.around(stage)
        for k, i in enumerate((behind, ahead)):
            self.near(stage, k, 1 - k, i).wait_recv()

    def complete(self, stage):
        opposite = self.around(stage)[2]
        for k in range(2):
            self.far(stage, k, opposite).wait_recv()

    def drain(self, stages=(0, 1)):
        for stage in stages:
            behind, ahead, _ = self.around(stage)
            for k, i in enumerate((behind, ahead)):
                for part in range(2):
                    self.near(stage, k, part, self.me[stage]).wait_send()
                self.far(stage, k, i).wait_send()


def kernel(
    request_ref, block_ref, length_ref, hid, gain_ref, w_hbm, pref, wo_hbm, bucket_ref, table_ref, out_ref,
    wbuf, hbuf, nbuf, acc, qkv, prefv, kvown, pbuf, tab, bias, tiles, wo, won, asend, aall,
    loc, own_s, sib_s, fwd_s, h_r, wz_s, wz_r, tb_s, tb_r, pz_s, pz_r, oz_s, oz_r,
    wt_s, wt_r, pt_s, pt_r, ot_s, ot_r, wn_s, wn_r, wf_s, wf_r, wb_s, wb_r, oc_s, oc_r, at_s, at_r,
):
    s = lax.axis_index("seq")
    t = lax.axis_index("tp")
    x, y, zh, c = s // 16, lax.rem(s // 4, 4), lax.rem(s // 2, 2), lax.rem(s, 2)
    side = t // 2
    leader = c == side
    inner = (t == 1) | (t == 2)
    beside = t + 1 - 2 * lax.rem(t, 2)
    across = lax.rem(t + 2, 4)
    group = lax.rem(t, 2) + 2 * c

    def at(zh_, c_, t_):
        return (((x * 4 + y) * 2 + zh_) * 2 + c_, t_)

    def column(x_, y_, c_):
        return (((x_ * 4 + y_) * 2 + zh) * 2 + c_, t)

    def along(step):
        other = lax.rem(zh * 4 + t + step + 8, 8)
        return at(other // 4, c, lax.rem(other, 4))

    x1, x3, y1, y3 = lax.rem(x + 1, 4), lax.rem(x + 3, 4), lax.rem(y + 1, 4), lax.rem(y + 3, 4)
    foreign = 1 - side
    xs, xf = [(column(x1, y, c_), column(x3, y, c_)) for c_ in (c, foreign)]
    ys, yf = [(column(x, y1, c_), column(x, y3, c_)) for c_ in (c, foreign)]
    core = at(zh, 1 - c, t)

    partners = [at(zh, lax.rem(c + dc, 2), lax.rem(t + dt, 4)) for dt in range(4) for dc in range(2) if dt or dc]
    partners += [at(1 - zh, c_, t_) for t_ in (t, across) for c_ in (c, 1 - c)]
    partners += [at(1 - zh, c, 3 - t)]
    partners += [
        (((x_ * 4 + y_) * 2 + zh) * 2 + c_, t)
        for x_, y_ in ((x1, y), (x3, y), (x, y1), (x, y3))
        for c_ in (c, 1 - c)
    ]
    barrier = pltpu.get_barrier_semaphore()
    for partner in partners:
        pl.semaphore_signal(barrier, inc=1, device_id=partner, device_id_type=MESH)

    load_pref = pltpu.make_async_copy(pref, prefv, loc.at[0])
    load_pref.start()
    load_own = pltpu.make_async_copy(hid, hbuf.at[pl.ds(aligned(t * ROWS, ROWS), ROWS)], loc.at[1])

    @pl.when(leader)
    def _():
        load_own.start()

    load_w = pltpu.make_async_copy(w_hbm, wbuf.at[0], loc.at[2])
    load_w.start()
    load_wo = pltpu.make_async_copy(wo_hbm, won, loc.at[3])
    load_wo.start()
    load_pref.wait()
    both = prefv[...].astype(jnp.float32)
    kvown[0] = both[:, 0, :].astype(jnp.bfloat16)
    kvown[1] = both[:, 1, :].astype(jnp.bfloat16)
    pl.semaphore_wait(barrier, len(partners))

    def weight_row(hh):
        return hh * 1024 + c * 128 + ((y * 256 + x * 32) if hh == 0 else (x * 256 + y * 32))

    def weight_piece(hh):
        rows = pl.ds(aligned(weight_row(hh), 32), 32)
        return remote(
            w_hbm.at[:, rows], wbuf.at[1, :, rows], wz_s.at[hh], wz_r.at[hh], along(2 if hh == 0 else -2)
        )

    def prefix_row(kv, zh_, c_):
        place = (y * 4 + x) if kv == 0 else (x * 4 + y)
        return pl.ds(aligned((place * 4 + zh_ * 2 + c_) * PB, PB), PB)

    def prefix_copy(target, kv, zh_, c_, to):
        rows = prefix_row(kv, zh_, c_)
        return remote(kvown.at[kv], pbuf.at[kv, rows], pz_s.at[target, kv], pz_r.at[zh_ * 2 + c_, kv], to)

    readers = (at(1 - zh, side, t), at(zh, side, across), at(1 - zh, side, across))
    own_prefix = [
        pltpu.make_async_copy(kvown.at[kv], pbuf.at[kv, prefix_row(kv, zh, c)], loc.at[4 + kv]) for kv in range(2)
    ]
    for kv in range(2):
        for k, reader in enumerate(readers):
            prefix_copy(k, kv, zh, c, reader).start()

        @pl.when(leader)
        def _():
            own_prefix[kv].start()

        @pl.when(jnp.logical_not(leader))
        def _():
            prefix_copy(3, kv, zh, c, core).start()

    send_table = remote(table_ref, tab, tb_s.at[0], tb_r.at[0], at(zh, c, across))
    send_table.start()
    for hh in range(2):
        weight_piece(hh).start()

    def quarter(k):
        j = jnp.where(t < 2, 2, 1)
        f = jnp.where(t < 2, 3, 0)
        return (t, beside, j, f)[k]

    def chunk(q, j):
        return hbuf.at[pl.ds(aligned(q * ROWS + j * CROWS, CROWS), CROWS)]

    own_to = at(zh, c, jnp.where(leader, beside, quarter(2)))

    def own_copy(j):
        return remote(hid.at[pl.ds(j * CROWS, CROWS)], chunk(t, j), own_s.at[j], h_r.at[t, j], own_to)

    for j in range(1):
        own_copy(j).start()

    def sibling_copy(k, j):
        q = quarter(k)
        src = hid.at[pl.ds(j * CROWS, CROWS)] if k == 0 else chunk(q, j)
        return remote(src, chunk(q, j), sib_s.at[k, j], h_r.at[q, j], core)

    def forward_copy(k, j):
        q = quarter(k)
        return remote(chunk(q, j), chunk(q, j), fwd_s.at[k, j], h_r.at[q, j], at(zh, c, beside))

    for j in range(CH):
        @pl.when(leader)
        def _():
            sibling_copy(0, j).start()

    def out_row(hh):
        return hh * 256 + c * 128 + ((y * 4 + x) if hh == 0 else (x * 4 + y)) * 8

    def out_piece(d, hh):
        rows = pl.ds(aligned(out_row(hh), 8), 8)
        step = (1, (2, -2)[hh], -1)[d - 1]
        return remote(wo_hbm.at[rows], wo.at[3 - d, rows], oz_s.at[d - 1, hh], oz_r.at[3 - d, hh], along(step))

    def arrive(k, j):
        @pl.when(leader)
        def _():
            sibling_copy(k, j).wait_recv()
            sibling_copy(k, j).start()

        if k >= 2:
            @pl.when(leader & inner)
            def _():
                forward_copy(k, j).start()

    def arrived(k):
        @pl.when(jnp.logical_not(leader))
        def _():
            for j in range(CH):
                sibling_copy(k, j).wait_recv()

    def tracks(views, columns, offs, unit, step, send, recv):
        first = Track(views[0], columns, offs[0], unit, step, (x, y), (xs, ys), send.at[0], recv.at[0])
        other = Track(views[1], columns, offs[1], unit, step, (y, x), (ys, xs), send.at[1], recv.at[1])
        return first, other

    w_view = lambda rows, columns: wbuf.at[1, :, rows, columns]
    o_view = lambda rows, columns: wo.at[:, rows, columns]
    w_tracks = tracks((w_view, w_view), COLS, (c * 128, 1024 + c * 128), 32, 256, wt_s, wt_r)
    p_tracks = tracks(
        (lambda rows, columns: pbuf.at[0, rows, columns], lambda rows, columns: pbuf.at[1, rows, columns]),
        COLS, (0, 0), 32, 128, pt_s, pt_r,
    )
    o_tracks = tracks((o_view, o_view), D, (c * 128, 256 + c * 128), 8, 32, ot_s, ot_r)

    places = ((y, y3, y1, yf), (x, x3, x1, xf))

    def w_region(hh, core_, i, part=None):
        rows = pl.ds(aligned(hh * 1024 + i * 256 + core_ * 128, 128), 128)
        half = COLS // 2
        return wbuf.at[1, :, rows, pl.ds(0, COLS) if part is None else pl.ds(part * half, half)]

    def w_near(hh, k, part, core_, i):
        region = w_region(hh, core_, i, part)
        return remote(region, region, wn_s.at[hh, k, part], wn_r.at[hh, core_, k, part], places[hh][3][k])

    def w_far(hh, k, core_, i):
        region = w_region(hh, core_, i, k)
        return remote(region, region, wf_s.at[hh, core_, k], wf_r.at[hh, core_, k], places[hh][3][k])

    def w_beside(hh, core_):
        region = w_region(hh, core_, places[hh][0])
        return remote(region, region, wb_s.at[hh], wb_r.at[hh], core)

    def w_first():
        for k, part in ((0, 0), (1, 1), (0, 1), (1, 0)):
            for hh in range(2):
                w_near(hh, k, part, c, places[hh][0]).start()

        @pl.when(leader)
        def _():
            for hh in range(2):
                w_beside(hh, c).start()

    def w_second():
        @pl.when(jnp.logical_not(leader))
        def _():
            for k in range(2):
                for hh in range(2):
                    for core_ in range(2):
                        w_near(hh, k, k, core_, places[hh][1 + k]).wait_recv()
                        w_far(hh, k, core_, places[hh][1 + k]).start()

    def w_rest():
        @pl.when(jnp.logical_not(leader))
        def _():
            for hh in range(2):
                w_beside(hh, 1 - c).wait_recv()
                for k in range(2):
                    for core_ in range(2):
                        w_near(hh, k, 1 - k, core_, places[hh][1 + k]).wait_recv()

    def w_complete():
        @pl.when(jnp.logical_not(leader))
        def _():
            for hh in range(2):
                for k in range(2):
                    for core_ in range(2):
                        w_far(hh, k, core_, lax.rem(places[hh][0] + 2, 4)).wait_recv()

    def core_out(hh, core_, i):
        region = wo.at[:, pl.ds(aligned(hh * 256 + core_ * 128 + i * 32, 32), 32)]
        return remote(region, region, oc_s.at[hh, i], oc_r.at[hh, i], core)

    def each(which, action, stage):
        for track in which:
            getattr(track, action)(stage)

    def norm(k):
        arrived(k)
        rows = pl.ds(aligned(quarter(k) * ROWS, ROWS), ROWS)
        gain = jnp.concatenate([gain_ref[i : i + 1, :].astype(jnp.float32) for i in range(D // 128)], 1)
        states = hbuf[rows, :].astype(jnp.float32)
        scale = lax.rsqrt(jnp.mean(states * states, -1, keepdims=True) + 1e-06)
        nbuf[rows, :] = (states * scale * gain).astype(jnp.bfloat16)

    def build_bias():
        bucket = jnp.concatenate([bucket_ref[i : i + 1, :] for i in range(DIST // 128)], 1)
        bucket = jnp.broadcast_to(bucket, (HEADS, DIST))
        table = jnp.where(leader, table_ref[...], tab[...])
        row = jnp.zeros((HEADS, DIST), jnp.float32)
        for b in range(BUCKETS):
            row = jnp.where(bucket == b, table[:, b : b + 1], row)
        bias[:, :PREFIX] = jnp.full((HEADS, PREFIX), NEG, jnp.float32)
        bias[:, PREFIX:] = row

    def build(h):
        for delta in range(5):
            window = jnp.broadcast_to(bias[h : h + 1, delta * 128 : delta * 128 + 256], (128, 256))
            rolled = pltpu.roll(window, 0, 1, stride=1, stride_axis=0)
            tiles[h // 2, delta, :, (h % 2) * 128 : (h % 2) * 128 + 128] = rolled[:, 128:]

    def prefix_arrived():
        for kv in range(2):
            for zh_ in range(2):
                for c_ in range(2):
                    mine = leader & (zh == zh_) & (c == c_)

                    @pl.when(jnp.logical_not(mine))
                    def _():
                        prefix_copy(0, kv, zh_, c_, core).wait_recv()

            @pl.when(leader)
            def _():
                own_prefix[kv].wait()

    prefix_arrived()
    each(p_tracks, "first", 0)
    for hh in range(2):
        weight_piece(hh).wait_recv()
    each(w_tracks, "first", 0)
    for j in range(1, CH):
        own_copy(j).start()
    for d in range(1, 4):
        for hh in range(2):
            out_piece(d, hh).start()
    each(p_tracks, "second", 0)
    each(p_tracks, "rest", 0)
    send_table.wait_recv()
    build_bias()
    each(w_tracks, "second", 0)
    each(p_tracks, "complete", 0)
    each(p_tracks, "first", 1)
    each(w_tracks, "rest", 0)
    each(w_tracks, "complete", 0)
    w_first()
    for j in range(2):
        arrive(1, j)
        arrive(2, j)
    build(0)
    each(p_tracks, "second", 1)
    for j in range(2, CH):
        arrive(1, j)
        arrive(2, j)

    @pl.when(leader)
    def _():
        load_own.wait()

    norm(0)
    for rho in range(3):
        for hh in range(2):
            out_piece(3 - rho, hh).wait_recv()
    each(o_tracks, "first", 0)
    w_second()
    for j in range(CH):
        arrive(3, j)
    build(1)
    build(2)
    each(o_tracks, "second", 0)
    norm(1)
    for h in range(3, HEADS):
        build(h)
    each(p_tracks, "rest", 1)
    each(p_tracks, "complete", 1)
    each(o_tracks, "rest", 0)
    norm(2)
    norm(3)
    each(o_tracks, "complete", 0)
    w_rest()
    load_w.wait()
    which = jnp.where(leader, 0, 1)

    def product(i, slices):
        total = None
        for hh, place in slices:
            rows = pl.ds(aligned(hh * 1024 + place * 256, 256), 256)
            part = jnp.dot(nbuf[:, rows], wbuf[which, i, rows, :], preferred_element_type=jnp.float32)
            total = part if total is None else total + part
        return total

    for i in range(3):
        acc[:, i * COLS : (i + 1) * COLS] = product(i, [(hh, places[hh][k]) for hh in range(2) for k in range(3)])
        if i == 0:
            each(o_tracks, "first", 1)
            for hh in range(2):
                core_out(hh, c, places[hh][0]).start()
    w_complete()
    for i in range(3):
        columns = slice(i * COLS, (i + 1) * COLS)
        far = product(i, [(hh, lax.rem(places[hh][0] + 2, 4)) for hh in range(2)])
        qkv[:, columns] = (acc[:, columns] + far).astype(jnp.bfloat16)

    slot = ((x * 4 + y) * 2 + zh) * 2 + side
    first_row = request_ref[slot] // RG * PREFIX
    lane = lax.broadcasted_iota(jnp.int32, (1, CACHE), 1)
    chosen = []
    for kv in range(2):
        target = jnp.zeros((1, CACHE), jnp.int32)
        for place in range(CACHE // PB):
            owner = (place // 4 % 4 * 4 + place // 16) * 4 + place % 4 if kv == 0 else place
            target = jnp.where(lane // PB == place, block_ref[owner] * PB, target)
        target = target + lane % PB - first_row
        match = lax.broadcasted_iota(jnp.int32, (PREFIX, CACHE), 0) == jnp.broadcast_to(target, (PREFIX, CACHE))
        pick = jnp.where(match, 1.0, 0.0).astype(jnp.bfloat16)
        chosen.append(jnp.dot(pick, pbuf[kv], preferred_element_type=jnp.float32).astype(jnp.bfloat16))

    low = lax.broadcasted_iota(jnp.int32, (128, 128), 1) < 64
    keys, values = [], []
    for p in range(HEADS // 2):
        lanes = slice(p * 128, p * 128 + 128)
        keys.append(chosen[0][:, lanes])
        values.append(
            jnp.concatenate([chosen[1][:, lanes], qkv[:, 2 * COLS + p * 128 : 2 * COLS + p * 128 + 128]], 0).T
        )

    def attend(r):
        for p in range(HEADS // 2):
            lanes = slice(p * 128, p * 128 + 128)
            query = qkv[r * 128 : r * 128 + 128, lanes]
            zero = jnp.zeros_like(query)
            stacked = jnp.concatenate([jnp.where(low, query, zero), jnp.where(low, zero, query)], 0)
            blocks = []
            for kb in range(r + 2):
                key = keys[p] if kb == 0 else qkv[kb * 128 - 128 : kb * 128, COLS + p * 128 : COLS + p * 128 + 128]
                part = lax.dot_general(key, stacked, (((1,), (1,)), ((), ())), preferred_element_type=jnp.float32)
                blocks.append(part + tiles[p, r + 1 - kb])
            top = functools.reduce(jnp.maximum, [jnp.max(b, 0, keepdims=True) for b in blocks])
            probs = [jnp.exp(b - top) for b in blocks]
            denom = functools.reduce(jnp.add, [jnp.sum(b, 0, keepdims=True) for b in probs])
            probs = jnp.concatenate([b.astype(jnp.bfloat16) for b in probs], 0)
            out = jnp.dot(values[p][:, : (r + 2) * 128], probs, preferred_element_type=jnp.float32) / denom
            pair = jnp.concatenate([out[:64, :128], out[64:, 128:]], 0)
            asend[r, :, lanes] = pair.T.astype(jnp.bfloat16)

    def attn_copy(r):
        return remote(asend.at[r], aall.at[group], at_s.at[r], at_r.at[group], at(zh, side, r))

    own_attn = pltpu.make_async_copy(asend.at[t], aall.at[group], loc.at[6])

    for r in (3, 0, 2, 1):
        attend(r)
        stays = leader & (t == r)

        @pl.when(stays)
        def _():
            own_attn.start()

        @pl.when(jnp.logical_not(stays))
        def _():
            attn_copy(r).start()

        if r == 3:
            each(o_tracks, "second", 1)
        if r == 2:
            each(o_tracks, "rest", 1)
            for hh in range(2):
                for k in range(2):
                    core_out(hh, c, places[hh][1 + k]).start()

    each(o_tracks, "complete", 1)
    for hh in range(2):
        core_out(hh, c, lax.rem(places[hh][0] + 2, 4)).start()
    for kv in range(2):
        for k, reader in enumerate(readers):
            prefix_copy(k, kv, zh, c, reader).wait_send()

        @pl.when(jnp.logical_not(leader))
        def _():
            prefix_copy(3, kv, zh, c, core).wait_send()

    send_table.wait_send()
    for hh in range(2):
        weight_piece(hh).wait_send()
        for d in range(1, 4):
            out_piece(d, hh).wait_send()
        for k in range(2):
            for part in range(2):
                w_near(hh, k, part, c, places[hh][0]).wait_send()
    for j in range(CH):
        own_copy(j).wait_send()

    @pl.when(leader)
    def _():
        for j in range(CH):
            for k in range(4):
                sibling_copy(k, j).wait_send()
        for hh in range(2):
            w_beside(hh, c).wait_send()

    @pl.when(jnp.logical_not(leader))
    def _():
        for hh in range(2):
            for k in range(2):
                for core_ in range(2):
                    w_far(hh, k, core_, places[hh][1 + k]).wait_send()

    @pl.when(leader & inner)
    def _():
        for j in range(CH):
            for k in range(2, 4):
                forward_copy(k, j).wait_send()

    for track in w_tracks:
        track.drain((0,))
    for track in (*p_tracks, *o_tracks):
        track.drain()
    load_wo.wait()
    for hh in range(2):
        for i in range(4):
            core_out(hh, 1 - c, i).wait_recv()

    def attn_arrived(g):
        remote(asend.at[0], aall.at[g], at_s.at[0], at_r.at[g], core).wait_recv()

    total = None
    for rho in range(-1, 3):
        g = lax.rem(t + 1 + rho, 4)
        if rho < 0:
            @pl.when(leader)
            def _():
                own_attn.wait()

            @pl.when(jnp.logical_not(leader))
            def _():
                attn_arrived(g)
        else:
            attn_arrived(g)
        weights = won[...] if rho < 0 else wo[rho]
        part = jnp.dot(aall[g], weights, preferred_element_type=jnp.float32)
        total = part if total is None else total + part
    length = length_ref[request_ref[s]]
    position = t * ROWS + lax.broadcasted_iota(jnp.int32, (ROWS, D), 0)
    out_ref[...] = jnp.where(position < length, total, 0.0).astype(jnp.bfloat16)
    for hh in range(2):
        for i in range(4):
            core_out(hh, c, i).wait_send()
    for r in range(TP):
        @pl.when(jnp.logical_not(leader & (t == r)))
        def _():
            attn_copy(r).wait_send()


def body(
    hidden,
    norm_gain,
    qkv_weight,
    out_weight,
    bias_table,
    prefix_cache,
    suffix_lengths,
    request_of_slot,
    block_of_slot,
    bias_bucket,
):
    vmem, smem = pl.BlockSpec(memory_space=pltpu.VMEM), pl.BlockSpec(memory_space=pltpu.SMEM)
    hbm = pl.BlockSpec(memory_space=pltpu.HBM)
    dma = pltpu.SemaphoreType.DMA
    bf16, f32 = jnp.bfloat16, jnp.float32
    out = pl.pallas_call(
        kernel,
        name="sublayer",
        out_shape=jax.ShapeDtypeStruct((ROWS, D), bf16),
        in_specs=[smem, smem, smem, hbm, vmem, hbm, hbm, hbm, vmem, vmem],
        out_specs=vmem,
        scratch_shapes=[
            pltpu.VMEM((2, 3, D, COLS), bf16),
            pltpu.VMEM((SLOT, D), bf16),
            pltpu.VMEM((SLOT, D), bf16),
            pltpu.VMEM((SLOT, 3 * COLS), f32),
            pltpu.VMEM((SLOT, 3 * COLS), bf16),
            pltpu.VMEM((PB, 2, COLS), bf16),
            pltpu.VMEM((2, PB, COLS), bf16),
            pltpu.VMEM((2, CACHE, COLS), bf16),
            pltpu.VMEM((HEADS, BUCKETS), f32),
            pltpu.VMEM((HEADS, PREFIX + DIST), f32),
            pltpu.VMEM((HEADS // 2, 5, 128, 256), f32),
            pltpu.VMEM((3, COLS, D), bf16),
            pltpu.VMEM((COLS, D), bf16),
            pltpu.VMEM((TP, ROWS, COLS), bf16),
            pltpu.VMEM((TP, ROWS, COLS), bf16),
            dma((7,)), dma((CH,)), dma((4, CH)), dma((4, CH)), dma((4, CH)),
            dma((2,)), dma((2,)), dma((1,)), dma((1,)), dma((4, 2)), dma((4, 2)), dma((3, 2)), dma((3, 2)),
            dma((2, 2, 6)), dma((2, 2, 6)), dma((2, 2, 6)), dma((2, 2, 6)), dma((2, 2, 6)), dma((2, 2, 6)),
            dma((2, 2, 2)), dma((2, 2, 2, 2)), dma((2, 2, 2)), dma((2, 2, 2)), dma((2,)), dma((2,)),
            dma((2, 4)), dma((2, 4)), dma((4,)), dma((4,)),
        ],
        compiler_params=pltpu.CompilerParams(collective_id=0, has_side_effects=True, vmem_limit_bytes=60 << 20),
    )(
        request_of_slot,
        block_of_slot,
        suffix_lengths,
        hidden[0],
        norm_gain.reshape(D // 128, 128),
        qkv_weight.transpose(1, 0, 2),
        prefix_cache,
        out_weight,
        bias_bucket.reshape(DIST // 128, 128),
        bias_table.T,
    )
    return out[None]


def solution(mesh):
    return jax.shard_map(
        body,
        mesh=mesh,
        in_specs=(
            P("seq", "tp", None),
            P(),
            P(None, None, "tp"),
            P("tp", None),
            P(None, "tp"),
            P("seq", None, "tp"),
            P(),
            P(),
            P(),
            P(),
        ),
        out_specs=P("seq", "tp", None),
        check_vma=False,
    )
```

```python
import functools

import jax
import jax.numpy as jnp
from jax import lax
from jax.experimental import pallas as pl
from jax.experimental.pallas import tpu as pltpu
from jax.sharding import PartitionSpec as P

MESH = pl.DeviceIdType.MESH
TP = 4
ROWS = 128
SLOT = ROWS * TP
D = 2048
COLS = 512
HEADS = 8
PB = 8
PREFIX = 128
CACHE = 512
DIST = 640
BUCKETS = 32
RG = 16
NEG = -1e30
CH = 4
CROWS = ROWS // CH


def aligned(start, unit):
    return pl.multiple_of(start, unit)


def remote(src, dst, send_sem, recv_sem, to):
    return pltpu.make_async_remote_copy(
        src_ref=src, dst_ref=dst, send_sem=send_sem, recv_sem=recv_sem, device_id=to, device_id_type=MESH
    )


class Track:
    def __init__(self, view, columns, off, unit, step, me, peers, send, recv):
        self.view, self.columns, self.off, self.unit, self.step = view, columns, off, unit, step
        self.me, self.peers, self.send, self.recv = me, peers, send, recv

    def region(self, stage, i, part=None):
        count = self.unit if stage == 0 else 4 * self.unit
        start = self.off + (self.me[1] * self.step + i * self.unit if stage == 0 else i * self.step)
        half = self.columns // 2
        columns = pl.ds(0, self.columns) if part is None else pl.ds(part * half, half)
        return self.view(pl.ds(aligned(start, self.unit), count), columns)

    def near(self, stage, k, part, i):
        region = self.region(stage, i, part)
        index = k * 2 + part
        return remote(region, region, self.send.at[stage, index], self.recv.at[stage, index], self.peers[stage][k])

    def far(self, stage, k, i):
        region = self.region(stage, i, k)
        return remote(region, region, self.send.at[stage, 4 + k], self.recv.at[stage, 4 + k], self.peers[stage][k])

    def around(self, stage):
        me = self.me[stage]
        return lax.rem(me + 3, 4), lax.rem(me + 1, 4), lax.rem(me + 2, 4)

    def first(self, stage):
        for k, part in ((0, 0), (1, 1), (0, 1), (1, 0)):
            self.near(stage, k, part, self.me[stage]).start()

    def second(self, stage):
        behind, ahead, _ = self.around(stage)
        for k, i in enumerate((behind, ahead)):
            self.near(stage, k, k, i).wait_recv()
            self.far(stage, k, i).start()

    def rest(self, stage):
        behind, ahead, _ = self.around(stage)
        for k, i in enumerate((behind, ahead)):
            self.near(stage, k, 1 - k, i).wait_recv()

    def complete(self, stage):
        opposite = self.around(stage)[2]
        for k in range(2):
            self.far(stage, k, opposite).wait_recv()

    def drain(self, stages=(0, 1)):
        for stage in stages:
            behind, ahead, _ = self.around(stage)
            for k, i in enumerate((behind, ahead)):
                for part in range(2):
                    self.near(stage, k, part, self.me[stage]).wait_send()
                self.far(stage, k, i).wait_send()


def kernel(
    request_ref, block_ref, length_ref, hid, gain_ref, w_hbm, pref, wo_hbm, bucket_ref, table_ref, out_ref,
    wbuf, hbuf, nbuf, acc, qkv, prefv, kvown, pbuf, tab, bias, tiles, wo, won, asend, aall,
    loc, own_s, sib_s, fwd_s, h_r, wz_s, wz_r, tb_s, tb_r, pz_s, pz_r, oz_s, oz_r,
    wt_s, wt_r, pt_s, pt_r, ot_s, ot_r, wn_s, wn_r, wf_s, wf_r, wb_s, wb_r, oc_s, oc_r, at_s, at_r,
):
    s = lax.axis_index("seq")
    t = lax.axis_index("tp")
    x, y, zh, c = s // 16, lax.rem(s // 4, 4), lax.rem(s // 2, 2), lax.rem(s, 2)
    side = t // 2
    leader = c == side
    inner = (t == 1) | (t == 2)
    beside = t + 1 - 2 * lax.rem(t, 2)
    across = lax.rem(t + 2, 4)
    group = lax.rem(t, 2) + 2 * c

    def at(zh_, c_, t_):
        return (((x * 4 + y) * 2 + zh_) * 2 + c_, t_)

    def column(x_, y_, c_):
        return (((x_ * 4 + y_) * 2 + zh) * 2 + c_, t)

    def along(step):
        other = lax.rem(zh * 4 + t + step + 8, 8)
        return at(other // 4, c, lax.rem(other, 4))

    x1, x3, y1, y3 = lax.rem(x + 1, 4), lax.rem(x + 3, 4), lax.rem(y + 1, 4), lax.rem(y + 3, 4)
    foreign = 1 - side
    xs, xf = [(column(x1, y, c_), column(x3, y, c_)) for c_ in (c, foreign)]
    ys, yf = [(column(x, y1, c_), column(x, y3, c_)) for c_ in (c, foreign)]
    core = at(zh, 1 - c, t)

    partners = [at(zh, lax.rem(c + dc, 2), lax.rem(t + dt, 4)) for dt in range(4) for dc in range(2) if dt or dc]
    partners += [at(1 - zh, c_, t_) for t_ in (t, across) for c_ in (c, 1 - c)]
    partners += [at(1 - zh, c, 3 - t)]
    partners += [
        (((x_ * 4 + y_) * 2 + zh) * 2 + c_, t)
        for x_, y_ in ((x1, y), (x3, y), (x, y1), (x, y3))
        for c_ in (c, 1 - c)
    ]
    barrier = pltpu.get_barrier_semaphore()
    for partner in partners:
        pl.semaphore_signal(barrier, inc=1, device_id=partner, device_id_type=MESH)

    load_pref = pltpu.make_async_copy(pref, prefv, loc.at[0])
    load_pref.start()
    load_own = pltpu.make_async_copy(hid, hbuf.at[pl.ds(aligned(t * ROWS, ROWS), ROWS)], loc.at[1])

    @pl.when(leader)
    def _():
        load_own.start()

    load_w = pltpu.make_async_copy(w_hbm, wbuf.at[0], loc.at[2])
    load_w.start()
    load_wo = pltpu.make_async_copy(wo_hbm, won, loc.at[3])
    load_wo.start()
    load_pref.wait()
    both = prefv[...].astype(jnp.float32)
    kvown[0] = both[:, 0, :].astype(jnp.bfloat16)
    kvown[1] = both[:, 1, :].astype(jnp.bfloat16)
    pl.semaphore_wait(barrier, len(partners))

    def weight_row(hh):
        return hh * 1024 + c * 128 + ((y * 256 + x * 32) if hh == 0 else (x * 256 + y * 32))

    def weight_piece(hh, part):
        rows = pl.ds(aligned(weight_row(hh), 32), 32)
        columns = pl.ds(part * (COLS // 2), COLS // 2)
        return remote(
            w_hbm.at[:, rows, columns],
            wbuf.at[1, :, rows, columns],
            wz_s.at[hh, part],
            wz_r.at[hh, part],
            along(2 if hh == 0 else -2),
        )

    def prefix_row(kv, zh_, c_):
        place = (y * 4 + x) if kv == 0 else (x * 4 + y)
        return pl.ds(aligned((place * 4 + zh_ * 2 + c_) * PB, PB), PB)

    def prefix_copy(target, kv, zh_, c_, to):
        rows = prefix_row(kv, zh_, c_)
        return remote(kvown.at[kv], pbuf.at[kv, rows], pz_s.at[target, kv], pz_r.at[zh_ * 2 + c_, kv], to)

    readers = (at(1 - zh, side, t), at(zh, side, across), at(1 - zh, side, across))
    own_prefix = [
        pltpu.make_async_copy(kvown.at[kv], pbuf.at[kv, prefix_row(kv, zh, c)], loc.at[4 + kv]) for kv in range(2)
    ]
    for kv in range(2):
        for k, reader in enumerate(readers):
            prefix_copy(k, kv, zh, c, reader).start()

        @pl.when(leader)
        def _():
            own_prefix[kv].start()

        @pl.when(jnp.logical_not(leader))
        def _():
            prefix_copy(3, kv, zh, c, core).start()

    send_table = remote(table_ref, tab, tb_s.at[0], tb_r.at[0], at(zh, c, across))
    send_table.start()
    for part in range(2):
        for hh in range(2):
            weight_piece(hh, part).start()

    def quarter(k):
        j = jnp.where(t < 2, 2, 1)
        f = jnp.where(t < 2, 3, 0)
        return (t, beside, j, f)[k]

    def chunk(q, j):
        return hbuf.at[pl.ds(aligned(q * ROWS + j * CROWS, CROWS), CROWS)]

    own_to = at(zh, c, jnp.where(leader, beside, quarter(2)))

    def own_copy(j):
        return remote(hid.at[pl.ds(j * CROWS, CROWS)], chunk(t, j), own_s.at[j], h_r.at[t, j], own_to)

    def sibling_copy(k, j):
        q = quarter(k)
        src = hid.at[pl.ds(j * CROWS, CROWS)] if k == 0 else chunk(q, j)
        return remote(src, chunk(q, j), sib_s.at[k, j], h_r.at[q, j], core)

    def forward_copy(k, j):
        q = quarter(k)
        return remote(chunk(q, j), chunk(q, j), fwd_s.at[k, j], h_r.at[q, j], at(zh, c, beside))

    for j in range(CH):
        @pl.when(leader)
        def _():
            sibling_copy(0, j).start()

    def out_row(hh):
        return hh * 256 + c * 128 + ((y * 4 + x) if hh == 0 else (x * 4 + y)) * 8

    def out_piece(d, hh):
        rows = pl.ds(aligned(out_row(hh), 8), 8)
        step = (1, (2, -2)[hh], -1)[d - 1]
        return remote(wo_hbm.at[rows], wo.at[3 - d, rows], oz_s.at[d - 1, hh], oz_r.at[3 - d, hh], along(step))

    def arrive(k, j, ends):
        @pl.when(leader & (inner != ends))
        def _():
            sibling_copy(k, j).wait_recv()
            sibling_copy(k, j).start()
            if k >= 2 and not ends:
                forward_copy(k, j).start()

    def arrived(k):
        @pl.when(jnp.logical_not(leader))
        def _():
            for j in range(CH):
                sibling_copy(k, j).wait_recv()

    def tracks(views, columns, offs, unit, step, send, recv):
        first = Track(views[0], columns, offs[0], unit, step, (x, y), (xs, ys), send.at[0], recv.at[0])
        other = Track(views[1], columns, offs[1], unit, step, (y, x), (ys, xs), send.at[1], recv.at[1])
        return first, other

    w_view = lambda rows, columns: wbuf.at[1, :, rows, columns]
    o_view = lambda rows, columns: wo.at[:, rows, columns]
    w_tracks = tracks((w_view, w_view), COLS, (c * 128, 1024 + c * 128), 32, 256, wt_s, wt_r)
    p_tracks = tracks(
        (lambda rows, columns: pbuf.at[0, rows, columns], lambda rows, columns: pbuf.at[1, rows, columns]),
        COLS, (0, 0), 32, 128, pt_s, pt_r,
    )
    o_tracks = tracks((o_view, o_view), D, (c * 128, 256 + c * 128), 8, 32, ot_s, ot_r)

    places = ((y, y3, y1, yf), (x, x3, x1, xf))

    def w_region(hh, core_, i, part=None):
        rows = pl.ds(aligned(hh * 1024 + i * 256 + core_ * 128, 128), 128)
        half = COLS // 2
        return wbuf.at[1, :, rows, pl.ds(0, COLS) if part is None else pl.ds(part * half, half)]

    def w_near(hh, k, part, core_, i):
        region = w_region(hh, core_, i, part)
        return remote(region, region, wn_s.at[hh, k, part], wn_r.at[hh, core_, k, part], places[hh][3][k])

    def w_far(hh, k, core_, i):
        region = w_region(hh, core_, i, k)
        return remote(region, region, wf_s.at[hh, core_, k], wf_r.at[hh, core_, k], places[hh][3][k])

    def w_beside(hh, core_):
        region = w_region(hh, core_, places[hh][0])
        return remote(region, region, wb_s.at[hh], wb_r.at[hh], core)

    def w_first():
        for k, part in ((0, 0), (1, 1), (0, 1), (1, 0)):
            for hh in range(2):
                w_near(hh, k, part, c, places[hh][0]).start()

        @pl.when(leader)
        def _():
            for hh in range(2):
                w_beside(hh, c).start()

    def w_second():
        @pl.when(jnp.logical_not(leader))
        def _():
            for k in range(2):
                for hh in range(2):
                    for core_ in range(2):
                        w_near(hh, k, k, core_, places[hh][1 + k]).wait_recv()
                        w_far(hh, k, core_, places[hh][1 + k]).start()

    def w_rest():
        @pl.when(jnp.logical_not(leader))
        def _():
            for hh in range(2):
                w_beside(hh, 1 - c).wait_recv()
                for k in range(2):
                    for core_ in range(2):
                        w_near(hh, k, 1 - k, core_, places[hh][1 + k]).wait_recv()

    def w_complete():
        @pl.when(jnp.logical_not(leader))
        def _():
            for hh in range(2):
                for k in range(2):
                    for core_ in range(2):
                        w_far(hh, k, core_, lax.rem(places[hh][0] + 2, 4)).wait_recv()

    def core_out(hh, core_, i):
        region = wo.at[:, pl.ds(aligned(hh * 256 + core_ * 128 + i * 32, 32), 32)]
        return remote(region, region, oc_s.at[hh, i], oc_r.at[hh, i], core)

    def each(which, action, stage):
        for track in which:
            getattr(track, action)(stage)

    def norm(k):
        arrived(k)
        rows = pl.ds(aligned(quarter(k) * ROWS, ROWS), ROWS)
        gain = jnp.concatenate([gain_ref[i : i + 1, :].astype(jnp.float32) for i in range(D // 128)], 1)
        states = hbuf[rows, :].astype(jnp.float32)
        scale = lax.rsqrt(jnp.mean(states * states, -1, keepdims=True) + 1e-06)
        nbuf[rows, :] = (states * scale * gain).astype(jnp.bfloat16)

    def build_bias():
        bucket = jnp.concatenate([bucket_ref[i : i + 1, :] for i in range(DIST // 128)], 1)
        bucket = jnp.broadcast_to(bucket, (HEADS, DIST))
        table = jnp.where(leader, table_ref[...], tab[...])
        row = jnp.zeros((HEADS, DIST), jnp.float32)
        for b in range(BUCKETS):
            row = jnp.where(bucket == b, table[:, b : b + 1], row)
        bias[:, :PREFIX] = jnp.full((HEADS, PREFIX), NEG, jnp.float32)
        bias[:, PREFIX:] = row

    def build(h):
        for delta in range(5):
            window = jnp.broadcast_to(bias[h : h + 1, delta * 128 : delta * 128 + 256], (128, 256))
            rolled = pltpu.roll(window, 0, 1, stride=1, stride_axis=0)
            tiles[h // 2, delta, :, (h % 2) * 128 : (h % 2) * 128 + 128] = rolled[:, 128:]

    def prefix_arrived():
        for kv in range(2):
            for zh_ in range(2):
                for c_ in range(2):
                    mine = leader & (zh == zh_) & (c == c_)

                    @pl.when(jnp.logical_not(mine))
                    def _():
                        prefix_copy(0, kv, zh_, c_, core).wait_recv()

            @pl.when(leader)
            def _():
                own_prefix[kv].wait()

    for d in range(1, 4):
        for hh in range(2):
            out_piece(d, hh).start()
    prefix_arrived()
    each(p_tracks, "first", 0)
    for part in range(2):
        for hh in range(2):
            weight_piece(hh, part).wait_recv()
        for k in (part, 1 - part):
            for track in w_tracks:
                track.near(0, k, part, track.me[0]).start()
    for j in range(CH):
        own_copy(j).start()
    each(p_tracks, "second", 0)
    each(p_tracks, "rest", 0)
    send_table.wait_recv()
    build_bias()
    each(w_tracks, "second", 0)
    for rho in range(3):
        for hh in range(2):
            out_piece(3 - rho, hh).wait_recv()
    each(o_tracks, "first", 0)
    each(p_tracks, "complete", 0)
    each(p_tracks, "first", 1)
    for k in range(1, 4):
        arrive(k, 0, False)
    each(w_tracks, "rest", 0)
    each(w_tracks, "complete", 0)
    w_first()
    each(o_tracks, "second", 0)
    for k in range(1, 4):
        arrive(k, 1, False)
    each(p_tracks, "second", 1)
    for j in range(2, CH):
        for k in range(1, 4):
            arrive(k, j, False)

    @pl.when(leader)
    def _():
        load_own.wait()

    norm(0)
    for h in range(4):
        build(h)
    for j in range(CH):
        for k in range(1, 4):
            arrive(k, j, True)
    w_second()
    each(o_tracks, "rest", 0)
    each(o_tracks, "complete", 0)
    each(o_tracks, "first", 1)
    for hh in range(2):
        core_out(hh, c, places[hh][0]).start()
    norm(1)
    for h in range(4, HEADS):
        build(h)
    each(p_tracks, "rest", 1)
    each(p_tracks, "complete", 1)
    norm(2)
    norm(3)
    w_rest()
    load_w.wait()
    which = jnp.where(leader, 0, 1)

    def product(i, slices):
        total = None
        for hh, place in slices:
            rows = pl.ds(aligned(hh * 1024 + place * 256, 256), 256)
            part = jnp.dot(nbuf[:, rows], wbuf[which, i, rows, :], preferred_element_type=jnp.float32)
            total = part if total is None else total + part
        return total

    for i in range(3):
        acc[:, i * COLS : (i + 1) * COLS] = product(i, [(hh, places[hh][k]) for hh in range(2) for k in range(3)])
    slot = ((x * 4 + y) * 2 + zh) * 2 + side
    first_row = request_ref[slot] // RG * PREFIX
    lane = lax.broadcasted_iota(jnp.int32, (1, CACHE), 1)
    chosen = []
    for kv in range(2):
        target = jnp.zeros((1, CACHE), jnp.int32)
        for place in range(CACHE // PB):
            owner = (place // 4 % 4 * 4 + place // 16) * 4 + place % 4 if kv == 0 else place
            target = jnp.where(lane // PB == place, block_ref[owner] * PB, target)
        target = target + lane % PB - first_row
        match = lax.broadcasted_iota(jnp.int32, (PREFIX, CACHE), 0) == jnp.broadcast_to(target, (PREFIX, CACHE))
        pick = jnp.where(match, 1.0, 0.0).astype(jnp.bfloat16)
        chosen.append(jnp.dot(pick, pbuf[kv], preferred_element_type=jnp.float32).astype(jnp.bfloat16))

    w_complete()
    for i in range(3):
        columns = slice(i * COLS, (i + 1) * COLS)
        far = product(i, [(hh, lax.rem(places[hh][0] + 2, 4)) for hh in range(2)])
        qkv[:, columns] = (acc[:, columns] + far).astype(jnp.bfloat16)

    low = lax.broadcasted_iota(jnp.int32, (128, 128), 1) < 64
    keys, values = [], []
    for p in range(HEADS // 2):
        lanes = slice(p * 128, p * 128 + 128)
        keys.append(chosen[0][:, lanes])
        values.append(
            jnp.concatenate([chosen[1][:, lanes], qkv[:, 2 * COLS + p * 128 : 2 * COLS + p * 128 + 128]], 0).T
        )

    def attend(r):
        for p in range(HEADS // 2):
            lanes = slice(p * 128, p * 128 + 128)
            query = qkv[r * 128 : r * 128 + 128, lanes]
            zero = jnp.zeros_like(query)
            stacked = jnp.concatenate([jnp.where(low, query, zero), jnp.where(low, zero, query)], 0)
            blocks = []
            for kb in range(r + 2):
                key = keys[p] if kb == 0 else qkv[kb * 128 - 128 : kb * 128, COLS + p * 128 : COLS + p * 128 + 128]
                part = lax.dot_general(key, stacked, (((1,), (1,)), ((), ())), preferred_element_type=jnp.float32)
                blocks.append(part + tiles[p, r + 1 - kb])
            top = functools.reduce(jnp.maximum, [jnp.max(b, 0, keepdims=True) for b in blocks])
            probs = [jnp.exp(b - top) for b in blocks]
            denom = functools.reduce(jnp.add, [jnp.sum(b, 0, keepdims=True) for b in probs])
            probs = jnp.concatenate([b.astype(jnp.bfloat16) for b in probs], 0)
            out = jnp.dot(values[p][:, : (r + 2) * 128], probs, preferred_element_type=jnp.float32) / denom
            pair = jnp.concatenate([out[:64, :128], out[64:, 128:]], 0)
            asend[r, :, lanes] = pair.T.astype(jnp.bfloat16)

    def attn_copy(r):
        return remote(asend.at[r], aall.at[group], at_s.at[r], at_r.at[group], at(zh, side, r))

    own_attn = pltpu.make_async_copy(asend.at[t], aall.at[group], loc.at[6])

    for r in (3, 0, 2, 1):
        attend(r)
        stays = leader & (t == r)

        @pl.when(stays)
        def _():
            own_attn.start()

        @pl.when(jnp.logical_not(stays))
        def _():
            attn_copy(r).start()

        if r == 3:
            each(o_tracks, "second", 1)
        if r == 2:
            each(o_tracks, "rest", 1)
            for hh in range(2):
                for k in range(2):
                    core_out(hh, c, places[hh][1 + k]).start()

    each(o_tracks, "complete", 1)
    for hh in range(2):
        core_out(hh, c, lax.rem(places[hh][0] + 2, 4)).start()
    for kv in range(2):
        for k, reader in enumerate(readers):
            prefix_copy(k, kv, zh, c, reader).wait_send()

        @pl.when(jnp.logical_not(leader))
        def _():
            prefix_copy(3, kv, zh, c, core).wait_send()

    send_table.wait_send()
    for hh in range(2):
        for part in range(2):
            weight_piece(hh, part).wait_send()
        for d in range(1, 4):
            out_piece(d, hh).wait_send()
        for k in range(2):
            for part in range(2):
                w_near(hh, k, part, c, places[hh][0]).wait_send()
    for j in range(CH):
        own_copy(j).wait_send()

    @pl.when(leader)
    def _():
        for j in range(CH):
            for k in range(4):
                sibling_copy(k, j).wait_send()
        for hh in range(2):
            w_beside(hh, c).wait_send()

    @pl.when(jnp.logical_not(leader))
    def _():
        for hh in range(2):
            for k in range(2):
                for core_ in range(2):
                    w_far(hh, k, core_, places[hh][1 + k]).wait_send()

    @pl.when(leader & inner)
    def _():
        for j in range(CH):
            for k in range(2, 4):
                forward_copy(k, j).wait_send()

    for track in w_tracks:
        track.drain((0,))
    for track in (*p_tracks, *o_tracks):
        track.drain()
    load_wo.wait()
    for hh in range(2):
        for i in range(4):
            core_out(hh, 1 - c, i).wait_recv()

    def attn_arrived(g):
        remote(asend.at[0], aall.at[g], at_s.at[0], at_r.at[g], core).wait_recv()

    total = None
    for rho in range(-1, 3):
        g = lax.rem(t + 1 + rho, 4)
        if rho < 0:
            @pl.when(leader)
            def _():
                own_attn.wait()

            @pl.when(jnp.logical_not(leader))
            def _():
                attn_arrived(g)
        else:
            attn_arrived(g)
        weights = won[...] if rho < 0 else wo[rho]
        part = jnp.dot(aall[g], weights, preferred_element_type=jnp.float32)
        total = part if total is None else total + part
    length = length_ref[request_ref[s]]
    position = t * ROWS + lax.broadcasted_iota(jnp.int32, (ROWS, D), 0)
    out_ref[...] = jnp.where(position < length, total, 0.0).astype(jnp.bfloat16)
    for hh in range(2):
        for i in range(4):
            core_out(hh, c, i).wait_send()
    for r in range(TP):
        @pl.when(jnp.logical_not(leader & (t == r)))
        def _():
            attn_copy(r).wait_send()


def body(
    hidden,
    norm_gain,
    qkv_weight,
    out_weight,
    bias_table,
    prefix_cache,
    suffix_lengths,
    request_of_slot,
    block_of_slot,
    bias_bucket,
):
    vmem, smem = pl.BlockSpec(memory_space=pltpu.VMEM), pl.BlockSpec(memory_space=pltpu.SMEM)
    hbm = pl.BlockSpec(memory_space=pltpu.HBM)
    dma = pltpu.SemaphoreType.DMA
    bf16, f32 = jnp.bfloat16, jnp.float32
    out = pl.pallas_call(
        kernel,
        name="sublayer",
        out_shape=jax.ShapeDtypeStruct((ROWS, D), bf16),
        in_specs=[smem, smem, smem, hbm, vmem, hbm, hbm, hbm, vmem, vmem],
        out_specs=vmem,
        scratch_shapes=[
            pltpu.VMEM((2, 3, D, COLS), bf16),
            pltpu.VMEM((SLOT, D), bf16),
            pltpu.VMEM((SLOT, D), bf16),
            pltpu.VMEM((SLOT, 3 * COLS), f32),
            pltpu.VMEM((SLOT, 3 * COLS), bf16),
            pltpu.VMEM((PB, 2, COLS), bf16),
            pltpu.VMEM((2, PB, COLS), bf16),
            pltpu.VMEM((2, CACHE, COLS), bf16),
            pltpu.VMEM((HEADS, BUCKETS), f32),
            pltpu.VMEM((HEADS, PREFIX + DIST), f32),
            pltpu.VMEM((HEADS // 2, 5, 128, 256), f32),
            pltpu.VMEM((3, COLS, D), bf16),
            pltpu.VMEM((COLS, D), bf16),
            pltpu.VMEM((TP, ROWS, COLS), bf16),
            pltpu.VMEM((TP, ROWS, COLS), bf16),
            dma((7,)), dma((CH,)), dma((4, CH)), dma((4, CH)), dma((4, CH)),
            dma((2, 2)), dma((2, 2)), dma((1,)), dma((1,)), dma((4, 2)), dma((4, 2)), dma((3, 2)), dma((3, 2)),
            dma((2, 2, 6)), dma((2, 2, 6)), dma((2, 2, 6)), dma((2, 2, 6)), dma((2, 2, 6)), dma((2, 2, 6)),
            dma((2, 2, 2)), dma((2, 2, 2, 2)), dma((2, 2, 2)), dma((2, 2, 2)), dma((2,)), dma((2,)),
            dma((2, 4)), dma((2, 4)), dma((4,)), dma((4,)),
        ],
        compiler_params=pltpu.CompilerParams(collective_id=0, has_side_effects=True, vmem_limit_bytes=60 << 20),
    )(
        request_of_slot,
        block_of_slot,
        suffix_lengths,
        hidden[0],
        norm_gain.reshape(D // 128, 128),
        qkv_weight.transpose(1, 0, 2),
        prefix_cache,
        out_weight,
        bias_bucket.reshape(DIST // 128, 128),
        bias_table.T,
    )
    return out[None]


def solution(mesh):
    return jax.shard_map(
        body,
        mesh=mesh,
        in_specs=(
            P("seq", "tp", None),
            P(),
            P(None, None, "tp"),
            P("tp", None),
            P(None, "tp"),
            P("seq", None, "tp"),
            P(),
            P(),
            P(),
            P(),
        ),
        out_specs=P("seq", "tp", None),
        check_vma=False,
    )
```

```python
import functools

import jax
import jax.numpy as jnp
from jax import lax
from jax.experimental import pallas as pl
from jax.experimental.pallas import tpu as pltpu
from jax.sharding import PartitionSpec as P

MESH = pl.DeviceIdType.MESH
TP = 4
ROWS = 128
SLOT = ROWS * TP
D = 2048
COLS = 512
HEADS = 8
PB = 8
PREFIX = 128
CACHE = 512
DIST = 640
BUCKETS = 32
RG = 16
NEG = -1e30
CH = 4
CROWS = ROWS // CH


def aligned(start, unit):
    return pl.multiple_of(start, unit)


def remote(src, dst, send_sem, recv_sem, to):
    return pltpu.make_async_remote_copy(
        src_ref=src, dst_ref=dst, send_sem=send_sem, recv_sem=recv_sem, device_id=to, device_id_type=MESH
    )


class Track:
    def __init__(self, view, columns, off, unit, step, me, peers, send, recv):
        self.view, self.columns, self.off, self.unit, self.step = view, columns, off, unit, step
        self.me, self.peers, self.send, self.recv = me, peers, send, recv

    def region(self, stage, i, part=None):
        count = self.unit if stage == 0 else 4 * self.unit
        start = self.off + (self.me[1] * self.step + i * self.unit if stage == 0 else i * self.step)
        half = self.columns // 2
        columns = pl.ds(0, self.columns) if part is None else pl.ds(part * half, half)
        return self.view(pl.ds(aligned(start, self.unit), count), columns)

    def near(self, stage, k, part, i):
        region = self.region(stage, i, part)
        index = k * 2 + part
        return remote(region, region, self.send.at[stage, index], self.recv.at[stage, index], self.peers[stage][k])

    def far(self, stage, k, i):
        region = self.region(stage, i, k)
        return remote(region, region, self.send.at[stage, 4 + k], self.recv.at[stage, 4 + k], self.peers[stage][k])

    def around(self, stage):
        me = self.me[stage]
        return lax.rem(me + 3, 4), lax.rem(me + 1, 4), lax.rem(me + 2, 4)

    def first(self, stage):
        for k, part in ((0, 0), (1, 1), (0, 1), (1, 0)):
            self.near(stage, k, part, self.me[stage]).start()

    def second(self, stage):
        behind, ahead, _ = self.around(stage)
        for k, i in enumerate((behind, ahead)):
            self.near(stage, k, k, i).wait_recv()
            self.far(stage, k, i).start()

    def rest(self, stage):
        behind, ahead, _ = self.around(stage)
        for k, i in enumerate((behind, ahead)):
            self.near(stage, k, 1 - k, i).wait_recv()

    def complete(self, stage):
        opposite = self.around(stage)[2]
        for k in range(2):
            self.far(stage, k, opposite).wait_recv()

    def drain(self, stages=(0, 1)):
        for stage in stages:
            behind, ahead, _ = self.around(stage)
            for k, i in enumerate((behind, ahead)):
                for part in range(2):
                    self.near(stage, k, part, self.me[stage]).wait_send()
                self.far(stage, k, i).wait_send()


def kernel(
    request_ref, block_ref, length_ref, hid, gain_ref, w_hbm, pref, wo_hbm, bucket_ref, table_ref, out_ref,
    wbuf, hbuf, nbuf, acc, qkv, prefv, kvown, pbuf, tab, bias, tiles, wo, won, asend, aall,
    loc, own_s, sib_s, fwd_s, h_r, wz_s, wz_r, tb_s, tb_r, pz_s, pz_r, oz_s, oz_r,
    wt_s, wt_r, pt_s, pt_r, ot_s, ot_r, wn_s, wn_r, wf_s, wf_r, wb_s, wb_r, oc_s, oc_r, at_s, at_r,
):
    s = lax.axis_index("seq")
    t = lax.axis_index("tp")
    x, y, zh, c = s // 16, lax.rem(s // 4, 4), lax.rem(s // 2, 2), lax.rem(s, 2)
    side = t // 2
    leader = c == side
    inner = (t == 1) | (t == 2)
    beside = t + 1 - 2 * lax.rem(t, 2)
    across = lax.rem(t + 2, 4)
    group = lax.rem(t, 2) + 2 * c

    def at(zh_, c_, t_):
        return (((x * 4 + y) * 2 + zh_) * 2 + c_, t_)

    def column(x_, y_, c_):
        return (((x_ * 4 + y_) * 2 + zh) * 2 + c_, t)

    def along(step):
        other = lax.rem(zh * 4 + t + step + 8, 8)
        return at(other // 4, c, lax.rem(other, 4))

    x1, x3, y1, y3 = lax.rem(x + 1, 4), lax.rem(x + 3, 4), lax.rem(y + 1, 4), lax.rem(y + 3, 4)
    foreign = 1 - side
    xs, xf = [(column(x1, y, c_), column(x3, y, c_)) for c_ in (c, foreign)]
    ys, yf = [(column(x, y1, c_), column(x, y3, c_)) for c_ in (c, foreign)]
    core = at(zh, 1 - c, t)

    partners = [at(zh, lax.rem(c + dc, 2), lax.rem(t + dt, 4)) for dt in range(4) for dc in range(2) if dt or dc]
    partners += [at(1 - zh, c_, t_) for t_ in (t, across) for c_ in (c, 1 - c)]
    partners += [at(1 - zh, c, 3 - t)]
    partners += [
        (((x_ * 4 + y_) * 2 + zh) * 2 + c_, t)
        for x_, y_ in ((x1, y), (x3, y), (x, y1), (x, y3))
        for c_ in (c, 1 - c)
    ]
    barrier = pltpu.get_barrier_semaphore()
    for partner in partners:
        pl.semaphore_signal(barrier, inc=1, device_id=partner, device_id_type=MESH)

    load_pref = pltpu.make_async_copy(pref, prefv, loc.at[0])
    load_pref.start()
    load_own = pltpu.make_async_copy(hid, hbuf.at[pl.ds(aligned(t * ROWS, ROWS), ROWS)], loc.at[1])

    @pl.when(leader)
    def _():
        load_own.start()

    load_w = pltpu.make_async_copy(w_hbm, wbuf.at[0], loc.at[2])
    load_w.start()
    load_wo = pltpu.make_async_copy(wo_hbm, won, loc.at[3])
    load_wo.start()
    load_pref.wait()
    both = prefv[...].astype(jnp.float32)
    kvown[0] = both[:, 0, :].astype(jnp.bfloat16)
    kvown[1] = both[:, 1, :].astype(jnp.bfloat16)
    pl.semaphore_wait(barrier, len(partners))

    def weight_row(hh):
        return hh * 1024 + c * 128 + ((y * 256 + x * 32) if hh == 0 else (x * 256 + y * 32))

    def weight_piece(hh, part):
        rows = pl.ds(aligned(weight_row(hh), 32), 32)
        columns = pl.ds(part * (COLS // 2), COLS // 2)
        return remote(
            w_hbm.at[:, rows, columns],
            wbuf.at[1, :, rows, columns],
            wz_s.at[hh, part],
            wz_r.at[hh, part],
            along(2 if hh == 0 else -2),
        )

    def prefix_row(kv, zh_, c_):
        place = (y * 4 + x) if kv == 0 else (x * 4 + y)
        return pl.ds(aligned((place * 4 + zh_ * 2 + c_) * PB, PB), PB)

    def prefix_copy(target, kv, zh_, c_, to):
        rows = prefix_row(kv, zh_, c_)
        return remote(kvown.at[kv], pbuf.at[kv, rows], pz_s.at[target, kv], pz_r.at[zh_ * 2 + c_, kv], to)

    readers = (at(1 - zh, side, t), at(zh, side, across), at(1 - zh, side, across))
    own_prefix = [
        pltpu.make_async_copy(kvown.at[kv], pbuf.at[kv, prefix_row(kv, zh, c)], loc.at[4 + kv]) for kv in range(2)
    ]
    for kv in range(2):
        for k, reader in enumerate(readers):
            prefix_copy(k, kv, zh, c, reader).start()

        @pl.when(leader)
        def _():
            own_prefix[kv].start()

        @pl.when(jnp.logical_not(leader))
        def _():
            prefix_copy(3, kv, zh, c, core).start()

    send_table = remote(table_ref, tab, tb_s.at[0], tb_r.at[0], at(zh, c, across))
    send_table.start()
    for part in range(2):
        for hh in range(2):
            weight_piece(hh, part).start()

    def quarter(k):
        j = jnp.where(t < 2, 2, 1)
        f = jnp.where(t < 2, 3, 0)
        return (t, beside, j, f)[k]

    def chunk(q, j):
        return hbuf.at[pl.ds(aligned(q * ROWS + j * CROWS, CROWS), CROWS)]

    own_to = at(zh, c, jnp.where(leader, beside, quarter(2)))

    def own_copy(j):
        return remote(hid.at[pl.ds(j * CROWS, CROWS)], chunk(t, j), own_s.at[j], h_r.at[t, j], own_to)

    def sibling_copy(k, j):
        q = quarter(k)
        src = hid.at[pl.ds(j * CROWS, CROWS)] if k == 0 else chunk(q, j)
        return remote(src, chunk(q, j), sib_s.at[k, j], h_r.at[q, j], core)

    def forward_copy(k, j):
        q = quarter(k)
        return remote(chunk(q, j), chunk(q, j), fwd_s.at[k, j], h_r.at[q, j], at(zh, c, beside))

    for j in range(CH):
        @pl.when(leader)
        def _():
            sibling_copy(0, j).start()

    def out_row(hh):
        return hh * 256 + c * 128 + ((y * 4 + x) if hh == 0 else (x * 4 + y)) * 8

    def out_piece(d, hh):
        rows = pl.ds(aligned(out_row(hh), 8), 8)
        step = (1, (2, -2)[hh], -1)[d - 1]
        return remote(wo_hbm.at[rows], wo.at[3 - d, rows], oz_s.at[d - 1, hh], oz_r.at[3 - d, hh], along(step))

    def arrive(k, j, ends):
        @pl.when(leader & (inner != ends))
        def _():
            sibling_copy(k, j).wait_recv()
            sibling_copy(k, j).start()
            if k >= 2 and not ends:
                forward_copy(k, j).start()

    def arrived(k):
        @pl.when(jnp.logical_not(leader))
        def _():
            for j in range(CH):
                sibling_copy(k, j).wait_recv()

    def tracks(views, columns, offs, unit, step, send, recv):
        first = Track(views[0], columns, offs[0], unit, step, (x, y), (xs, ys), send.at[0], recv.at[0])
        other = Track(views[1], columns, offs[1], unit, step, (y, x), (ys, xs), send.at[1], recv.at[1])
        return first, other

    w_view = lambda rows, columns: wbuf.at[1, :, rows, columns]
    o_view = lambda rows, columns: wo.at[:, rows, columns]
    w_tracks = tracks((w_view, w_view), COLS, (c * 128, 1024 + c * 128), 32, 256, wt_s, wt_r)
    p_tracks = tracks(
        (lambda rows, columns: pbuf.at[0, rows, columns], lambda rows, columns: pbuf.at[1, rows, columns]),
        COLS, (0, 0), 32, 128, pt_s, pt_r,
    )
    o_tracks = tracks((o_view, o_view), D, (c * 128, 256 + c * 128), 8, 32, ot_s, ot_r)

    places = ((y, y3, y1, yf), (x, x3, x1, xf))

    def w_region(hh, core_, i, part=None):
        rows = pl.ds(aligned(hh * 1024 + i * 256 + core_ * 128, 128), 128)
        half = COLS // 2
        return wbuf.at[1, :, rows, pl.ds(0, COLS) if part is None else pl.ds(part * half, half)]

    def w_near(hh, k, part, core_, i):
        region = w_region(hh, core_, i, part)
        return remote(region, region, wn_s.at[hh, k, part], wn_r.at[hh, core_, k, part], places[hh][3][k])

    def w_far(hh, k, core_, i):
        region = w_region(hh, core_, i, k)
        return remote(region, region, wf_s.at[hh, core_, k], wf_r.at[hh, core_, k], places[hh][3][k])

    def w_beside(hh, core_):
        region = w_region(hh, core_, places[hh][0])
        return remote(region, region, wb_s.at[hh], wb_r.at[hh], core)

    def w_first():
        for k, part in ((0, 0), (1, 1), (0, 1), (1, 0)):
            for hh in range(2):
                w_near(hh, k, part, c, places[hh][0]).start()

        @pl.when(leader)
        def _():
            for hh in range(2):
                w_beside(hh, c).start()

    def w_second():
        @pl.when(jnp.logical_not(leader))
        def _():
            for k in range(2):
                for hh in range(2):
                    for core_ in range(2):
                        w_near(hh, k, k, core_, places[hh][1 + k]).wait_recv()
                        w_far(hh, k, core_, places[hh][1 + k]).start()

    def w_rest():
        @pl.when(jnp.logical_not(leader))
        def _():
            for hh in range(2):
                w_beside(hh, 1 - c).wait_recv()
                for k in range(2):
                    for core_ in range(2):
                        w_near(hh, k, 1 - k, core_, places[hh][1 + k]).wait_recv()

    def w_complete():
        @pl.when(jnp.logical_not(leader))
        def _():
            for hh in range(2):
                for k in range(2):
                    for core_ in range(2):
                        w_far(hh, k, core_, lax.rem(places[hh][0] + 2, 4)).wait_recv()

    def core_out(hh, core_, i):
        region = wo.at[:, pl.ds(aligned(hh * 256 + core_ * 128 + i * 32, 32), 32)]
        return remote(region, region, oc_s.at[hh, i], oc_r.at[hh, i], core)

    def each(which, action, stage):
        for track in which:
            getattr(track, action)(stage)

    def norm(k):
        arrived(k)
        rows = pl.ds(aligned(quarter(k) * ROWS, ROWS), ROWS)
        gain = jnp.concatenate([gain_ref[i : i + 1, :].astype(jnp.float32) for i in range(D // 128)], 1)
        states = hbuf[rows, :].astype(jnp.float32)
        scale = lax.rsqrt(jnp.mean(states * states, -1, keepdims=True) + 1e-06)
        nbuf[rows, :] = (states * scale * gain).astype(jnp.bfloat16)

    def build_bias():
        bucket = jnp.concatenate([bucket_ref[i : i + 1, :] for i in range(DIST // 128)], 1)
        bucket = jnp.broadcast_to(bucket, (HEADS, DIST))
        table = jnp.where(leader, table_ref[...], tab[...])
        row = jnp.zeros((HEADS, DIST), jnp.float32)
        for b in range(BUCKETS):
            row = jnp.where(bucket == b, table[:, b : b + 1], row)
        bias[:, :PREFIX] = jnp.full((HEADS, PREFIX), NEG, jnp.float32)
        bias[:, PREFIX:] = row

    def build(h):
        for delta in range(5):
            window = jnp.broadcast_to(bias[h : h + 1, delta * 128 : delta * 128 + 256], (128, 256))
            rolled = pltpu.roll(window, 0, 1, stride=1, stride_axis=0)
            tiles[h // 2, delta, :, (h % 2) * 128 : (h % 2) * 128 + 128] = rolled[:, 128:]

    def prefix_arrived():
        for kv in range(2):
            for zh_ in range(2):
                for c_ in range(2):
                    mine = leader & (zh == zh_) & (c == c_)

                    @pl.when(jnp.logical_not(mine))
                    def _():
                        prefix_copy(0, kv, zh_, c_, core).wait_recv()

            @pl.when(leader)
            def _():
                own_prefix[kv].wait()

    for d in range(1, 4):
        for hh in range(2):
            out_piece(d, hh).start()
    prefix_arrived()
    each(p_tracks, "first", 0)
    for part in range(2):
        for hh in range(2):
            weight_piece(hh, part).wait_recv()
        for k in (part, 1 - part):
            for track in w_tracks:
                track.near(0, k, part, track.me[0]).start()
    for j in range(CH):
        own_copy(j).start()
    each(p_tracks, "second", 0)
    each(p_tracks, "rest", 0)
    send_table.wait_recv()
    build_bias()
    each(w_tracks, "second", 0)
    for rho in range(3):
        for hh in range(2):
            out_piece(3 - rho, hh).wait_recv()
    each(o_tracks, "first", 0)
    each(p_tracks, "complete", 0)
    each(p_tracks, "first", 1)
    for k in range(1, 4):
        arrive(k, 0, False)
    each(w_tracks, "rest", 0)
    each(w_tracks, "complete", 0)
    w_first()
    each(o_tracks, "second", 0)
    for k in range(1, 4):
        arrive(k, 1, False)
    each(p_tracks, "second", 1)
    for j in range(2, CH):
        for k in range(1, 4):
            arrive(k, j, False)

    @pl.when(leader)
    def _():
        load_own.wait()

    norm(0)
    for h in range(4):
        build(h)
    for j in range(CH):
        for k in range(1, 4):
            arrive(k, j, True)
    w_second()
    each(o_tracks, "rest", 0)
    each(o_tracks, "complete", 0)
    each(o_tracks, "first", 1)
    for hh in range(2):
        core_out(hh, c, places[hh][0]).start()
    norm(1)
    for h in range(4, HEADS):
        build(h)
    each(p_tracks, "rest", 1)
    each(p_tracks, "complete", 1)
    norm(2)
    norm(3)
    w_rest()
    load_w.wait()
    which = jnp.where(leader, 0, 1)

    def product(i, slices):
        total = None
        for hh, place in slices:
            rows = pl.ds(aligned(hh * 1024 + place * 256, 256), 256)
            part = jnp.dot(nbuf[:, rows], wbuf[which, i, rows, :], preferred_element_type=jnp.float32)
            total = part if total is None else total + part
        return total

    for i in range(3):
        acc[:, i * COLS : (i + 1) * COLS] = product(i, [(hh, places[hh][k]) for hh in range(2) for k in range(3)])
    slot = ((x * 4 + y) * 2 + zh) * 2 + side
    first_row = request_ref[slot] // RG * PREFIX
    lane = lax.broadcasted_iota(jnp.int32, (1, CACHE), 1)
    chosen = []
    for kv in range(2):
        target = jnp.zeros((1, CACHE), jnp.int32)
        for place in range(CACHE // PB):
            owner = (place // 4 % 4 * 4 + place // 16) * 4 + place % 4 if kv == 0 else place
            target = jnp.where(lane // PB == place, block_ref[owner] * PB, target)
        target = target + lane % PB - first_row
        match = lax.broadcasted_iota(jnp.int32, (PREFIX, CACHE), 0) == jnp.broadcast_to(target, (PREFIX, CACHE))
        pick = jnp.where(match, 1.0, 0.0).astype(jnp.bfloat16)
        chosen.append(jnp.dot(pick, pbuf[kv], preferred_element_type=jnp.float32).astype(jnp.bfloat16))

    w_complete()
    for i in range(3):
        columns = slice(i * COLS, (i + 1) * COLS)
        far = product(i, [(hh, lax.rem(places[hh][0] + 2, 4)) for hh in range(2)])
        qkv[:, columns] = (acc[:, columns] + far).astype(jnp.bfloat16)

    low = lax.broadcasted_iota(jnp.int32, (128, 128), 1) < 64
    keys, values = [], []
    for p in range(HEADS // 2):
        lanes = slice(p * 128, p * 128 + 128)
        keys.append(chosen[0][:, lanes])
        values.append(
            jnp.concatenate([chosen[1][:, lanes], qkv[:, 2 * COLS + p * 128 : 2 * COLS + p * 128 + 128]], 0).T
        )

    def attend(r):
        pairs = range(HEADS // 2)
        scores = []
        for p in pairs:
            lanes = slice(p * 128, p * 128 + 128)
            query = qkv[r * 128 : r * 128 + 128, lanes]
            zero = jnp.zeros_like(query)
            stacked = jnp.concatenate([jnp.where(low, query, zero), jnp.where(low, zero, query)], 0)
            blocks = []
            for kb in range(r + 2):
                key = keys[p] if kb == 0 else qkv[kb * 128 - 128 : kb * 128, COLS + p * 128 : COLS + p * 128 + 128]
                part = lax.dot_general(key, stacked, (((1,), (1,)), ((), ())), preferred_element_type=jnp.float32)
                blocks.append(part + tiles[p, r + 1 - kb])
            scores.append(blocks)
        weighed = []
        for blocks in scores:
            top = functools.reduce(jnp.maximum, [jnp.max(b, 0, keepdims=True) for b in blocks])
            probs = [jnp.exp(b - top) for b in blocks]
            denom = functools.reduce(jnp.add, [jnp.sum(b, 0, keepdims=True) for b in probs])
            weighed.append((jnp.concatenate([b.astype(jnp.bfloat16) for b in probs], 0), denom))
        for p in pairs:
            probs, denom = weighed[p]
            out = jnp.dot(values[p][:, : (r + 2) * 128], probs, preferred_element_type=jnp.float32) * (1.0 / denom)
            pair = jnp.concatenate([out[:64, :128], out[64:, 128:]], 0)
            asend[r, :, p * 128 : p * 128 + 128] = pair.T.astype(jnp.bfloat16)

    def attn_copy(r):
        return remote(asend.at[r], aall.at[group], at_s.at[r], at_r.at[group], at(zh, side, r))

    own_attn = pltpu.make_async_copy(asend.at[t], aall.at[group], loc.at[6])

    for r in (3, 0, 2, 1):
        attend(r)
        stays = leader & (t == r)

        @pl.when(stays)
        def _():
            own_attn.start()

        @pl.when(jnp.logical_not(stays))
        def _():
            attn_copy(r).start()

        if r == 3:
            each(o_tracks, "second", 1)
        if r == 2:
            each(o_tracks, "rest", 1)
            for hh in range(2):
                for k in range(2):
                    core_out(hh, c, places[hh][1 + k]).start()

    each(o_tracks, "complete", 1)
    for hh in range(2):
        core_out(hh, c, lax.rem(places[hh][0] + 2, 4)).start()
    for kv in range(2):
        for k, reader in enumerate(readers):
            prefix_copy(k, kv, zh, c, reader).wait_send()

        @pl.when(jnp.logical_not(leader))
        def _():
            prefix_copy(3, kv, zh, c, core).wait_send()

    send_table.wait_send()
    for hh in range(2):
        for part in range(2):
            weight_piece(hh, part).wait_send()
        for d in range(1, 4):
            out_piece(d, hh).wait_send()
        for k in range(2):
            for part in range(2):
                w_near(hh, k, part, c, places[hh][0]).wait_send()
    for j in range(CH):
        own_copy(j).wait_send()

    @pl.when(leader)
    def _():
        for j in range(CH):
            for k in range(4):
                sibling_copy(k, j).wait_send()
        for hh in range(2):
            w_beside(hh, c).wait_send()

    @pl.when(jnp.logical_not(leader))
    def _():
        for hh in range(2):
            for k in range(2):
                for core_ in range(2):
                    w_far(hh, k, core_, places[hh][1 + k]).wait_send()

    @pl.when(leader & inner)
    def _():
        for j in range(CH):
            for k in range(2, 4):
                forward_copy(k, j).wait_send()

    for track in w_tracks:
        track.drain((0,))
    for track in (*p_tracks, *o_tracks):
        track.drain()
    load_wo.wait()
    for hh in range(2):
        for i in range(4):
            core_out(hh, 1 - c, i).wait_recv()

    def attn_arrived(g):
        remote(asend.at[0], aall.at[g], at_s.at[0], at_r.at[g], core).wait_recv()

    total = None
    for rho in range(-1, 3):
        g = lax.rem(t + 1 + rho, 4)
        if rho < 0:
            @pl.when(leader)
            def _():
                own_attn.wait()

            @pl.when(jnp.logical_not(leader))
            def _():
                attn_arrived(g)
        else:
            attn_arrived(g)
        weights = won[...] if rho < 0 else wo[rho]
        part = jnp.dot(aall[g], weights, preferred_element_type=jnp.float32)
        total = part if total is None else total + part
    length = length_ref[request_ref[s]]
    position = t * ROWS + lax.broadcasted_iota(jnp.int32, (ROWS, D), 0)
    out_ref[...] = jnp.where(position < length, total, 0.0).astype(jnp.bfloat16)
    for hh in range(2):
        for i in range(4):
            core_out(hh, c, i).wait_send()
    for r in range(TP):
        @pl.when(jnp.logical_not(leader & (t == r)))
        def _():
            attn_copy(r).wait_send()


def body(
    hidden,
    norm_gain,
    qkv_weight,
    out_weight,
    bias_table,
    prefix_cache,
    suffix_lengths,
    request_of_slot,
    block_of_slot,
    bias_bucket,
):
    vmem, smem = pl.BlockSpec(memory_space=pltpu.VMEM), pl.BlockSpec(memory_space=pltpu.SMEM)
    hbm = pl.BlockSpec(memory_space=pltpu.HBM)
    dma = pltpu.SemaphoreType.DMA
    bf16, f32 = jnp.bfloat16, jnp.float32
    out = pl.pallas_call(
        kernel,
        name="sublayer",
        out_shape=jax.ShapeDtypeStruct((ROWS, D), bf16),
        in_specs=[smem, smem, smem, hbm, vmem, hbm, hbm, hbm, vmem, vmem],
        out_specs=vmem,
        scratch_shapes=[
            pltpu.VMEM((2, 3, D, COLS), bf16),
            pltpu.VMEM((SLOT, D), bf16),
            pltpu.VMEM((SLOT, D), bf16),
            pltpu.VMEM((SLOT, 3 * COLS), f32),
            pltpu.VMEM((SLOT, 3 * COLS), bf16),
            pltpu.VMEM((PB, 2, COLS), bf16),
            pltpu.VMEM((2, PB, COLS), bf16),
            pltpu.VMEM((2, CACHE, COLS), bf16),
            pltpu.VMEM((HEADS, BUCKETS), f32),
            pltpu.VMEM((HEADS, PREFIX + DIST), f32),
            pltpu.VMEM((HEADS // 2, 5, 128, 256), f32),
            pltpu.VMEM((3, COLS, D), bf16),
            pltpu.VMEM((COLS, D), bf16),
            pltpu.VMEM((TP, ROWS, COLS), bf16),
            pltpu.VMEM((TP, ROWS, COLS), bf16),
            dma((7,)), dma((CH,)), dma((4, CH)), dma((4, CH)), dma((4, CH)),
            dma((2, 2)), dma((2, 2)), dma((1,)), dma((1,)), dma((4, 2)), dma((4, 2)), dma((3, 2)), dma((3, 2)),
            dma((2, 2, 6)), dma((2, 2, 6)), dma((2, 2, 6)), dma((2, 2, 6)), dma((2, 2, 6)), dma((2, 2, 6)),
            dma((2, 2, 2)), dma((2, 2, 2, 2)), dma((2, 2, 2)), dma((2, 2, 2)), dma((2,)), dma((2,)),
            dma((2, 4)), dma((2, 4)), dma((4,)), dma((4,)),
        ],
        compiler_params=pltpu.CompilerParams(collective_id=0, has_side_effects=True, vmem_limit_bytes=60 << 20),
    )(
        request_of_slot,
        block_of_slot,
        suffix_lengths,
        hidden[0],
        norm_gain.reshape(D // 128, 128),
        qkv_weight.transpose(1, 0, 2),
        prefix_cache,
        out_weight,
        bias_bucket.reshape(DIST // 128, 128),
        bias_table.T,
    )
    return out[None]


def solution(mesh):
    return jax.shard_map(
        body,
        mesh=mesh,
        in_specs=(
            P("seq", "tp", None),
            P(),
            P(None, None, "tp"),
            P("tp", None),
            P(None, "tp"),
            P("seq", None, "tp"),
            P(),
            P(),
            P(),
            P(),
        ),
        out_specs=P("seq", "tp", None),
        check_vma=False,
    )
```
